32 devices in a mesh: rep: 8 (over y, x, core), shard: 4 (over z).
Axes of the slice: x: 2, y: 2, z: 4, core: 2. Of those that a mesh axis runs over, the one named last changes fastest.
Arguments:
- tokens: bfloat16 [16384, 768], P(('rep', 'shard')), may hold values from -6 to 6
- ln1_scale: bfloat16 [768], P('shard'), may hold values from 0.5 to 1.5
- ln1_shift: bfloat16 [768], P('shard'), may hold values from -1.75 to 1.75
- w_query: bfloat16 [768, 768], P('shard'), may hold values from -0.21875 to 0.21875
- b_query: bfloat16 [768], P('shard'), may hold values from -1.75 to 1.75
- w_key: bfloat16 [768, 768], P('shard'), may hold values from -0.21875 to 0.21875
- b_key: bfloat16 [768], P('shard'), may hold values from -1.75 to 1.75
- w_value: bfloat16 [768, 768], P('shard'), may hold values from -0.21875 to 0.21875
- b_value: bfloat16 [768], P('shard'), may hold values from -1.75 to 1.75
- shift_taps: bfloat16 [768, 64], P('shard'), may hold values from -0.75 to 0.75
- ssm_coef: bfloat16 [768, 64], P('shard'), may hold values from -0.125 to 0.125
- ssm_rate: bfloat16 [768, 64], P('shard'), may hold values from 0.0009994507 to 0.099609375
- ssm_skip: bfloat16 [768], P('shard'), may hold values from 0.25 to 1.75
- w_out: bfloat16 [768, 768], P('shard'), may hold values from -0.21875 to 0.21875
- b_out: bfloat16 [768], P('shard'), may hold values from -1.75 to 1.75
- ln2_scale: bfloat16 [768], P('shard'), may hold values from 0.5 to 1.5
- ln2_shift: bfloat16 [768], P('shard'), may hold values from -1.75 to 1.75
- w_up: bfloat16 [768, 3072], P('shard'), may hold values from -0.21875 to 0.21875
- b_up: bfloat16 [3072], P('shard'), may hold values from -1.75 to 1.75
- w_down: bfloat16 [3072, 768], P('shard'), may hold values from -0.109375 to 0.109375
- b_down: bfloat16 [768], P('shard'), may hold values from -1.75 to 1.75
- cotangent: bfloat16 [16384, 768], P(('rep', 'shard')), may hold values from -6 to 6
- piece_slot: int32 [1024], replicated, may hold values from 0 to 1023, as said below
- lengths: int32 [32, 4], P(('rep', 'shard')), may hold values from 64 to 320, as said below
Outputs:
- block_output: bfloat16 [16384, 768], P(('rep', 'shard'))
- grad_tokens: bfloat16 [16384, 768], P(('rep', 'shard'))
- grad_ln1_scale: float32 [768], P('shard')
- grad_ln1_shift: float32 [768], P('shard')
- grad_w_query: float32 [768, 768], P('shard')
- grad_b_query: float32 [768], P('shard')
- grad_w_key: float32 [768, 768], P('shard')
- grad_b_key: float32 [768], P('shard')
- grad_w_value: float32 [768, 768], P('shard')
- grad_b_value: float32 [768], P('shard')
- grad_shift_taps: float32 [768, 64], P('shard')
- grad_ssm_coef: float32 [768, 64], P('shard')
- grad_ssm_rate: float32 [768, 64], P('shard')
- grad_ssm_skip: float32 [768], P('shard')
- grad_w_out: float32 [768, 768], P('shard')
- grad_b_out: float32 [768], P('shard')
- grad_ln2_scale: float32 [768], P('shard')
- grad_ln2_shift: float32 [768], P('shard')
- grad_w_up: float32 [768, 3072], P('shard')
- grad_b_up: float32 [3072], P('shard')
- grad_w_down: float32 [3072, 768], P('shard')
- grad_b_down: float32 [768], P('shard')
The draws below stay inside these ranges and needn't reach their ends.
Inputs may be any that keep to these rules, and one draw needn't show every extreme that they name: piece_slot is a permutation of the slots; the 32 pieces of each device in the given order go one to each buffer (piece_slot // 32 takes every value once in each aligned block of 32 entries). `lengths`: each row holds one sequence of 320 tokens and three of 64 tokens, in some order (multiples of 64 that sum to 512).
All inputs are finite; a program needn't handle non-finite values.
Results may differ from the reference program's by a relative error of at most 0.02.
Values may be sent and summed in bfloat16 or wider, within the bound.
A program may use at most 256 MiB of HBM per device.

```python
import math
import jax
import jax.numpy as jnp
from jax import lax

D = 768
FF = 3072
NSTATE = 64
SHIFT = 64
TOK_DEV = 512
SEQ_DEV = 4
SLOTS = 32
TOKENS = 16384
N_REP = 8
N_SHARD = 4


def permutation_rows(key, count):
    subkeys = jax.random.split(key, count)
    return jax.vmap(lambda subkey: jax.random.permutation(subkey, count))(subkeys)


def draw_piece_slot(key, part):
    target = permutation_rows(jax.random.fold_in(key, 3), SLOTS)
    landing = permutation_rows(jax.random.fold_in(key, 5), SLOTS)
    sources = jnp.broadcast_to(jnp.arange(SLOTS)[:, None], (SLOTS, SLOTS))
    arrival = landing[target, sources]
    return (target * SLOTS + arrival).reshape(-1).astype(jnp.int32)


def length_row(subkey):
    block_count = TOK_DEV // SHIFT
    longest = block_count * 5 // 8
    remain = block_count - longest
    first_key, second_key = jax.random.split(subkey)
    cut_picks = jax.random.permutation(first_key, remain - 1)[:SEQ_DEV - 2] + 1
    cut_points = jnp.sort(cut_picks).astype(jnp.int32)
    bounds = jnp.concatenate([jnp.zeros((1,), jnp.int32), cut_points, jnp.full((1,), remain, jnp.int32)])
    part_sizes = bounds[1:] - bounds[:-1]
    length_list = jnp.concatenate([jnp.full((1,), longest, jnp.int32), part_sizes])
    return length_list[jax.random.permutation(second_key, SEQ_DEV)] * SHIFT


def draw_lengths(key, part):
    subkeys = jax.random.split(jax.random.fold_in(key, 7), SLOTS)
    return jax.vmap(length_row)(subkeys).astype(jnp.int32)


def level_of(rng, shape, cuts, least, largest):
    def one(position, parts):
        steps = jax.random.uniform(jax.random.fold_in(jax.random.fold_in(rng, 6), position), (parts,), jnp.float32, least / len(cuts), largest / len(cuts))
        return jnp.repeat(jnp.exp(steps), shape[position] // parts).reshape((-1,) + (1,) * (len(shape) - position - 1))

    gain = one(*cuts[0])
    for cut in cuts[1:]:
        gain = gain * one(*cut)
    return gain


def bell_draw(own_key, dims, deviation, bound, cuts=(), held_as=jnp.bfloat16):
    gain = level_of(own_key, dims, cuts, -0.22, 0.18) if cuts else 1.0
    values = jax.random.normal(own_key, dims, jnp.float32) * deviation * gain
    return jnp.minimum(jnp.maximum(values, -bound), bound).astype(held_as)


def setup_inputs(seed: int = 0) -> dict:
    key_of = jax.random.split(jax.random.key(seed), 25)
    return {
        "tokens": bell_draw(key_of[0], (TOKENS, D), 1.0, 6.0, ((0, 32),)),
        "ln1_scale": jnp.clip(1.0 + 0.1 * jax.random.normal(key_of[1], (D,), jnp.float32), 0.5, 1.5).astype(jnp.bfloat16),
        "ln1_shift": bell_draw(key_of[2], (D,), 0.3, 1.75, ((0, 4),)),
        "w_query": bell_draw(key_of[3], (D, D), D ** -0.5, 0.21875, ((0, 4),)),
        "b_query": bell_draw(key_of[4], (D,), 0.3, 1.75, ((0, 4),)),
        "w_key": bell_draw(key_of[5], (D, D), D ** -0.5, 0.21875, ((0, 4),)),
        "b_key": bell_draw(key_of[6], (D,), 0.3, 1.75, ((0, 4),)),
        "w_value": bell_draw(key_of[7], (D, D), D ** -0.5, 0.21875, ((0, 4),)),
        "b_value": bell_draw(key_of[8], (D,), 0.3, 1.75, ((0, 4),)),
        "shift_taps": bell_draw(key_of[9], (D, SHIFT), SHIFT ** -0.5, 0.75, ((0, 4),)),
        "ssm_coef": bell_draw(key_of[10], (D, NSTATE), 0.02, 0.125, ((0, 4),)),
        "ssm_rate": jnp.clip(jnp.exp(math.log(0.099609375) - 4.6018058 * jax.random.uniform(key_of[11], (D, NSTATE), jnp.float32) ** level_of(key_of[11], (D, NSTATE), ((0, 4),), -0.2, 0.2)), 0.0009994507, 0.099609375).astype(jnp.bfloat16),
        "ssm_skip": jnp.clip(1.0 + 0.15 * jax.random.normal(key_of[12], (D,), jnp.float32), 0.25, 1.75).astype(jnp.bfloat16),
        "w_out": bell_draw(key_of[13], (D, D), D ** -0.5, 0.21875, ((0, 4),)),
        "b_out": bell_draw(key_of[14], (D,), 0.3, 1.75, ((0, 4),)),
        "ln2_scale": jnp.clip(1.0 + 0.1 * jax.random.normal(key_of[15], (D,), jnp.float32), 0.5, 1.5).astype(jnp.bfloat16),
        "ln2_shift": bell_draw(key_of[16], (D,), 0.3, 1.75, ((0, 4),)),
        "w_up": bell_draw(key_of[17], (D, FF), D ** -0.5, 0.21875, ((0, 4),)),
        "b_up": bell_draw(key_of[18], (FF,), 0.3, 1.75, ((0, 4),)),
        "w_down": bell_draw(key_of[19], (FF, D), FF ** -0.5, 0.109375, ((0, 4),)),
        "b_down": bell_draw(key_of[20], (D,), 0.3, 1.75, ((0, 4),)),
        "cotangent": bell_draw(key_of[21], (TOKENS, D), 1.0, 6.0, ((0, 32),)),
        "piece_slot": draw_piece_slot(jax.random.fold_in(key_of[24], 71), 0),
        "lengths": draw_lengths(jax.random.fold_in(key_of[24], 71), 0),
    }


PRECISE = lax.Precision.HIGHEST
EPSILON = 1e-05

@jax.custom_vjp
def low(v):
    return lax.optimization_barrier(v.astype(jnp.bfloat16)).astype(jnp.float32)

@jax.custom_vjp
def low_back(v):
    return v

def low_keep(v):
    return (low(v), None)

def low_pass(kept, grad):
    return (grad,)

def back_keep(v):
    return (v, None)

def back_low(kept, grad):
    return (low(grad),)
low.defvjp(low_keep, low_pass)
low_back.defvjp(back_keep, back_low)

def rounded_both(v):
    return low(low_back(v))

def layer_norm(values_in, scale_in, shift_in):
    average = lax.optimization_barrier(jnp.mean(values_in, axis=-1, keepdims=True))
    centred = values_in - average
    spread = lax.optimization_barrier(jnp.mean(centred * centred, axis=-1, keepdims=True))
    return centred * lax.rsqrt(spread + EPSILON) * scale_in + shift_in

def smooth_gate(values_in):
    return jax.nn.gelu(values_in, approximate=True)

def toeplitz_tables(tap_count):
    lag_index = lax.broadcasted_iota(jnp.int32, (tap_count, tap_count, tap_count), 0)
    row_index = lax.broadcasted_iota(jnp.int32, (tap_count, tap_count, tap_count), 1)
    col_index = lax.broadcasted_iota(jnp.int32, (tap_count, tap_count, tap_count), 2)
    lower_band = jnp.where(row_index - col_index == lag_index, 1.0, 0.0).astype(jnp.float32)
    upper_band = jnp.where(row_index - col_index + tap_count == lag_index, 1.0, 0.0).astype(jnp.float32)
    return (lower_band, upper_band)

def mixing(key_blocks, value_blocks, shift_taps, ssm_coef, ssm_rate, ssm_skip, carried):
    tap_count = shift_taps.shape[1]
    lower_band, upper_band = toeplitz_tables(tap_count)
    keys_low = rounded_both(key_blocks)
    near_taps = rounded_both(jnp.einsum('cj,jab->cab', shift_taps, lower_band, precision=PRECISE))
    far_taps = rounded_both(jnp.einsum('cj,jab->cab', shift_taps, upper_band, precision=PRECISE))
    before = jnp.concatenate([jnp.zeros_like(keys_low[:1]), keys_low[:-1]], axis=0)
    shifted = jnp.einsum('cab,ibc->iac', near_taps, keys_low, precision=PRECISE)
    shifted = shifted + carried[:, None, None] * jnp.einsum('cab,ibc->iac', far_taps, before, precision=PRECISE)
    inputs = shifted * value_blocks
    inputs_low = rounded_both(inputs)
    lag_steps = jnp.arange(tap_count).astype(jnp.float32)
    decay_table = jnp.exp(-ssm_rate[:, :, None] * lag_steps[None, None, :])
    kernel = jnp.einsum('cn,cnm->cm', ssm_coef, decay_table, precision=PRECISE)
    inner_band = rounded_both(jnp.einsum('cm,mab->cab', kernel, lower_band, precision=PRECISE))
    within = jnp.einsum('cab,ibc->iac', inner_band, inputs_low, precision=PRECISE)
    tail_decay = rounded_both(jnp.flip(decay_table, axis=2))
    local_state = jnp.einsum('cnb,ibc->icn', tail_decay, inputs_low, precision=PRECISE)
    block_decay = jnp.exp(-ssm_rate * tap_count)

    def advance(carried_state, step_input):
        fresh_state, keep_flag = step_input
        next_state = keep_flag * block_decay * carried_state + fresh_state
        return (next_state, carried_state)
    _, previous = lax.scan(advance, jnp.zeros_like(local_state[0]), (local_state, carried))
    previous_low = rounded_both(previous)
    lead_decay = rounded_both(ssm_coef[:, :, None] * decay_table * jnp.exp(-ssm_rate)[:, :, None])
    across = carried[:, None, None] * jnp.einsum('cna,icn->iac', lead_decay, previous_low, precision=PRECISE)
    return within + across + ssm_skip * inputs

def carry_flags(length_list, block_count, tap_count):
    block_sizes = length_list // tap_count
    start_blocks = jnp.cumsum(block_sizes) - block_sizes
    block_ids = jnp.arange(block_count)
    opening = jnp.any(block_ids[:, None] == start_blocks[None, :], axis=1)
    return jnp.where(opening, 0.0, 1.0).astype(jnp.float32)

def layer_block(tokens_in, weights, carried):
    ln1_scale, ln1_shift, w_query, b_query, w_key, b_key, w_value, b_value, shift_taps, ssm_coef, ssm_rate, ssm_skip, w_out, b_out, ln2_scale, ln2_shift, w_up, b_up, w_down, b_down = weights
    tap_count = shift_taps.shape[1]
    model_dim = tokens_in.shape[1]
    block_count = tokens_in.shape[0] // tap_count
    normed = low(layer_norm(tokens_in, ln1_scale, ln1_shift))
    queries = low_back(jnp.dot(normed, w_query, precision=PRECISE, preferred_element_type=jnp.float32) + b_query)
    key_proj = low_back(jnp.dot(normed, w_key, precision=PRECISE, preferred_element_type=jnp.float32) + b_key)
    value_proj = low_back(jnp.dot(normed, w_value, precision=PRECISE, preferred_element_type=jnp.float32) + b_value)
    mixed_out = mixing(key_proj.reshape(block_count, tap_count, model_dim), value_proj.reshape(block_count, tap_count, model_dim), shift_taps, ssm_coef, ssm_rate, ssm_skip, carried)
    gated = low(queries * mixed_out.reshape(tokens_in.shape))
    branch = low_back(jnp.dot(gated, w_out, precision=PRECISE, preferred_element_type=jnp.float32) + b_out)
    middle = tokens_in + branch
    normed_two = low(layer_norm(middle, ln2_scale, ln2_shift))
    hidden = low_back(jnp.dot(normed_two, w_up, precision=PRECISE, preferred_element_type=jnp.float32) + b_up)
    active = low(smooth_gate(hidden))
    result = low_back(jnp.dot(active, w_down, precision=PRECISE, preferred_element_type=jnp.float32) + b_down)
    return middle + result

def reference(tokens, ln1_scale, ln1_shift, w_query, b_query, w_key, b_key, w_value, b_value, shift_taps, ssm_coef, ssm_rate, ssm_skip, w_out, b_out, ln2_scale, ln2_shift, w_up, b_up, w_down, b_down, cotangent, piece_slot, lengths):
    slot_count = N_REP * N_SHARD
    model_dim = tokens.shape[1]
    piece_rows = tokens.shape[0] // (slot_count * slot_count)
    tap_count = shift_taps.shape[1]
    block_count = tokens.shape[0] // slot_count // tap_count
    arrival_order = jnp.argsort(piece_slot).astype(jnp.int32)

    def to_balanced(array):
        pieces = array.reshape(slot_count * slot_count, piece_rows, model_dim)
        return pieces[arrival_order].reshape(slot_count, -1, model_dim)

    def to_given(array):
        pieces = array.reshape(slot_count * slot_count, piece_rows, model_dim)
        return pieces[piece_slot].reshape(-1, model_dim)
    params = (ln1_scale.astype(jnp.float32), ln1_shift.astype(jnp.float32), w_query.astype(jnp.float32), b_query.astype(jnp.float32), w_key.astype(jnp.float32), b_key.astype(jnp.float32), w_value.astype(jnp.float32), b_value.astype(jnp.float32), shift_taps.astype(jnp.float32), ssm_coef.astype(jnp.float32), ssm_rate.astype(jnp.float32), ssm_skip.astype(jnp.float32), w_out.astype(jnp.float32), b_out.astype(jnp.float32), ln2_scale.astype(jnp.float32), ln2_shift.astype(jnp.float32), w_up.astype(jnp.float32), b_up.astype(jnp.float32), w_down.astype(jnp.float32), b_down.astype(jnp.float32))
    balanced = to_balanced(tokens).astype(jnp.float32)
    carry_all = jax.vmap(lambda length_list: carry_flags(length_list, block_count, tap_count))(lengths)

    def forward(inputs_all, weights):

        def per_buffer(step_input):
            return layer_block(step_input[0], weights, step_input[1])
        return lax.map(jax.checkpoint(per_buffer), (inputs_all, carry_all))
    output, pullback = jax.vjp(forward, balanced, params)
    grad_input, grad_params = pullback(to_balanced(cotangent).astype(jnp.float32))
    g_ln1_scale, g_ln1_shift, g_w_query, g_b_query, g_w_key, g_b_key, g_w_value, g_b_value, g_shift_taps, g_ssm_coef, g_ssm_rate, g_ssm_skip, g_w_out, g_b_out, g_ln2_scale, g_ln2_shift, g_w_up, g_b_up, g_w_down, g_b_down = grad_params
    block_output = to_given(output).astype(jnp.bfloat16)
    grad_tokens = to_given(grad_input).astype(jnp.bfloat16)
    return (block_output, grad_tokens, g_ln1_scale, g_ln1_shift, g_w_query, g_b_query, g_w_key, g_b_key, g_w_value, g_b_value, g_shift_taps, g_ssm_coef, g_ssm_rate, g_ssm_skip, g_w_out, g_b_out, g_ln2_scale, g_ln2_shift, g_w_up, g_b_up, g_w_down, g_b_down)
```

```python
import jax
import jax.numpy as jnp
from jax import lax
from jax.experimental import pallas as pl
from jax.experimental.pallas import tpu as pltpu
from jax.sharding import PartitionSpec as P

EPSILON = 1e-05
GELU_A = 0.7978845608028654
GELU_B = 0.044715


def to_float(array):
    return array.astype(jnp.float32)


def to_half(array):
    return array.astype(jnp.bfloat16)


def dot_nn(one, two, out=jnp.float32):
    return jnp.dot(one, two, preferred_element_type=jnp.float32).astype(out)


def dot_tn(one, two, out=jnp.float32):
    return lax.dot_general(
        one, two, (((0,), (0,)), ((), ())), preferred_element_type=jnp.float32
    ).astype(out)


def dot_nt(one, two, out=jnp.float32):
    return lax.dot_general(
        one, two, (((1,), (1,)), ((), ())), preferred_element_type=jnp.float32
    ).astype(out)


MESH = pl.DeviceIdType.MESH


class Place:
    def __init__(self, rep_count, shard_count):
        self.rep_count, self.shard_count = rep_count, shard_count
        self.rep, self.shard = lax.axis_index("rep"), lax.axis_index("shard")

    def by_rep(self, mask):
        return (lax.bitwise_xor(self.rep, mask), self.shard)

    def by_shard(self, mask):
        return (self.rep, lax.bitwise_xor(self.shard, mask))

    def bit(self, mask):
        return lax.bitwise_and(lax.div(self.rep, mask), 1)

    def partners(self):
        found, mask = [], 1
        while mask < self.rep_count:
            found.append(self.by_rep(mask))
            mask *= 2
        return found + [self.by_shard(k) for k in range(1, self.shard_count)]

    def meet(self):
        barrier = pltpu.get_barrier_semaphore()
        partners = self.partners()
        for device in partners:
            pl.semaphore_signal(barrier, inc=1, device_id=device, device_id_type=MESH)
        pl.semaphore_wait(barrier, len(partners))


def plane_masks(rep_count, order):
    masks, mask = [], 2
    while mask < rep_count:
        masks.append(mask)
        mask *= 2
    return masks if order == 0 else masks[::-1]


def offset_of(index, masks):
    total = 0
    for i, mask in enumerate(masks):
        if (index >> i) & 1:
            total |= mask
    return total


def remote(source, target, sems, index, device):
    send, receive = sems
    return pltpu.make_async_remote_copy(
        src_ref=source,
        dst_ref=target,
        send_sem=send.at[index],
        recv_sem=receive.at[index],
        device_id=device,
        device_id_type=MESH,
    )


AHEAD = 3


def gather_body(rep_count, shard_count, units, *refs):
    tensors = 1 + max(tensor for tensor, _ in units)
    locals_, pack = refs[:tensors], refs[tensors]
    outs, pack_out = refs[tensors + 1 : 2 * tensors + 1], refs[2 * tensors + 1]
    held, send, receive, pack_send, pack_receive, done = refs[2 * tensors + 2 :]
    place = Place(rep_count, shard_count)
    place.meet()
    me, shard = place.rep, place.shard
    others = shard_count - 1
    stages = len(plane_masks(rep_count, 0)) + 1
    width = others + stages
    keep = []

    small = []
    for k in range(1, shard_count):
        copy = remote(
            pack, pack_out.at[shard], (pack_send, pack_receive), k - 1, place.by_shard(k)
        )
        copy.start()
        small.append(copy)
    own = pltpu.make_async_copy(pack, pack_out.at[shard], done.at[tensors])
    own.start()
    for tensor in range(tensors):
        pltpu.make_async_copy(
            locals_[tensor], outs[tensor].at[shard], done.at[tensor]
        ).start()

    def across(unit):
        tensor, pick = units[unit]
        copies = []
        for k in range(1, shard_count):
            copies.append(
                remote(
                    pick(locals_[tensor].at[me]),
                    held.at[unit, 0, k - 1],
                    (send, receive),
                    unit * width + k - 1,
                    place.by_shard(k),
                )
            )
        return copies

    def doubling(unit, stage):
        masks = plane_masks(rep_count, unit % 2) + [1]
        count = 1 << stage
        return remote(
            held.at[unit, pl.ds(0, count)],
            held.at[unit, pl.ds(count, count)],
            (send, receive),
            unit * width + others + stage,
            place.by_rep(masks[stage]),
        )

    def write(unit, first, count):
        tensor, pick = units[unit]
        masks = plane_masks(rep_count, unit % 2) + [1]
        for m in range(first, first + count):
            piece = lax.bitwise_xor(me, offset_of(m, masks))
            for k in range(1, shard_count):
                pltpu.make_async_copy(
                    held.at[unit, m, k - 1],
                    pick(outs[tensor].at[lax.bitwise_xor(shard, k), piece]),
                    done.at[tensor],
                ).start()

    flights = {}
    total = len(units)
    for unit in range(min(AHEAD, total)):
        flights[unit, -1] = across(unit)
        for copy in flights[unit, -1]:
            copy.start()
    for step in range(total + stages):
        for stage in range(stages, -1, -1):
            unit = step - stage
            if not 0 <= unit < total:
                continue
            if stage == 0:
                for copy in flights[unit, -1]:
                    copy.wait_recv()
                if unit + AHEAD < total:
                    flights[unit + AHEAD, -1] = across(unit + AHEAD)
                    for copy in flights[unit + AHEAD, -1]:
                        copy.start()
            else:
                flights[unit, stage - 1].wait_recv()
            if stage < stages:
                flights[unit, stage] = doubling(unit, stage)
                flights[unit, stage].start()
            if stage == 0:
                write(unit, 0, 1)
            else:
                write(unit, 1 << (stage - 1), 1 << (stage - 1))
    for copy in small:
        copy.wait()
    own.wait()
    for unit in range(total):
        for copy in flights[unit, -1]:
            copy.wait_send()
        for stage in range(stages):
            flights[unit, stage].wait_send()
    for tensor in range(tensors):
        pltpu.make_async_copy(outs[tensor], outs[tensor], done.at[tensor]).wait()


def gather_weights(squares, up, down, pack, rep_count, shard_count):
    rows, width = squares[0].shape
    piece = rows // rep_count
    parts = up.shape[1] // width
    locals_ = [w.reshape(rep_count, piece, width) for w in squares]
    locals_.append(up.reshape(rep_count, piece, up.shape[1]))
    locals_.append(down.reshape(rep_count, parts, piece, width))
    units = [(i, lambda ref: ref) for i in range(len(squares))]
    for q in range(parts):
        units.append((len(squares), lambda ref, q=q: ref.at[:, pl.ds(q * width, width)]))
    for q in range(parts):
        units.append((len(squares) + 1, lambda ref, q=q: ref.at[q]))
    anywhere = pl.BlockSpec(memory_space=pl.ANY)
    copies = len(units) * (shard_count + len(plane_masks(rep_count, 0)))
    outs = [jax.ShapeDtypeStruct((shard_count,) + w.shape, w.dtype) for w in locals_ + [pack]]
    found = pl.pallas_call(
        lambda *refs: gather_body(rep_count, shard_count, units, *refs),
        in_specs=[anywhere] * (len(locals_) + 1),
        out_specs=[anywhere] * len(outs),
        out_shape=outs,
        scratch_shapes=[
            pltpu.VMEM((len(units), rep_count, shard_count - 1, piece, width), jnp.bfloat16),
            pltpu.SemaphoreType.DMA((copies,)),
            pltpu.SemaphoreType.DMA((copies,)),
            pltpu.SemaphoreType.DMA((shard_count - 1,)),
            pltpu.SemaphoreType.DMA((shard_count - 1,)),
            pltpu.SemaphoreType.DMA((len(outs),)),
        ],
        compiler_params=pltpu.CompilerParams(
            collective_id=0, has_side_effects=True, vmem_limit_bytes=40 * 1024 * 1024
        ),
        cost_estimate=pl.CostEstimate(flops=0, bytes_accessed=200_000_000, transcendentals=0),
        name="gather_weights",
    )(*locals_, pack)
    whole = [w.reshape(shard_count * rows, width) for w in found[: len(squares)]]
    whole.append(found[-3].reshape(shard_count * rows, up.shape[1]))
    whole.append(found[-2].reshape(shard_count * down.shape[0], width))
    return whole, found[-1]


def add_into(target, other, count):
    def step(i, unused):
        target[i] = to_half(to_float(target[i]) + to_float(other[i]))
        return unused

    lax.fori_loop(0, count, step, 0)


class Reduction:
    def __init__(self, place, order, source, half, came, back, sems, base, write):
        self.place, self.source, self.half, self.came, self.back = place, source, half, came, back
        self.sems, self.base, self.write = sems, base, write
        self.masks = plane_masks(place.rep_count, order)
        self.flight = None
        self.kept = None
        self.sent = []
        self.rest = place.rep_count // 2

    def start(self):
        place = self.place
        core = place.bit(1)
        self.kept = pltpu.make_async_copy(
            self.source.at[:, :, core], self.half, self.sems[2].at[self.base]
        )
        self.kept.start()
        self.fly(self.source.at[:, :, 1 - core], self.came[0], 0, place.by_rep(1))

    def fly(self, source, target, index, device):
        copy = remote(source, target, self.sems[:2], self.base + index, device)
        copy.start()
        self.sent.append(copy)
        self.flight = copy

    def steps(self):
        place = self.place
        shards = place.shard_count
        count = len(self.masks)
        todo = []

        def after_core():
            self.kept.wait()
            self.flight.wait_recv()
            half, came = self.half, self.came[0]

            def step(i, unused):
                for j in range(self.rest):
                    half[i, j] = to_half(to_float(half[i, j]) + to_float(came[i, j]))
                return unused

            lax.fori_loop(0, shards, step, 0)
            leave(0)

        def index_of(chosen):
            free = [mask for mask in plane_masks(place.rep_count, 0) if mask not in chosen]
            spots = []
            for bits in range(1 << len(free)):
                spot = 0
                for i, mask in enumerate(free):
                    if (bits >> i) & 1:
                        spot += mask // 2
                spots.append(spot)
            return spots

        def own_spot(chosen):
            total = 0
            for mask in chosen:
                total = total + place.bit(mask) * (mask // 2)
            return total

        def leave(stage):
            mask = self.masks[stage]
            chosen = self.masks[: stage + 1]
            base = own_spot(self.masks[:stage]) + (1 - place.bit(mask)) * (mask // 2)
            self.group = []
            for n, spot in enumerate(index_of(chosen)):
                copy = remote(
                    self.half.at[:, base + spot],
                    self.came[1 + stage].at[n],
                    self.sems[:2],
                    self.base + 1 + stage * self.rest + n,
                    place.by_rep(mask),
                )
                copy.start()
                self.sent.append(copy)
                self.group.append(copy)

        def after_plane(stage):
            mask = self.masks[stage]
            chosen = self.masks[: stage + 1]
            base = own_spot(chosen)
            spots = index_of(chosen)
            for copy in self.group:
                copy.wait_recv()
            half, came = self.half, self.came[1 + stage]

            def step(i, unused):
                for n, spot in enumerate(spots):
                    at = base + spot
                    half[i, at] = to_half(to_float(half[i, at]) + to_float(came[n, i]))
                return unused

            lax.fori_loop(0, shards, step, 0)
            if stage + 1 < count:
                leave(stage + 1)
                return
            self.group = []
            for k in range(1, shards):
                copy = remote(
                    self.half.at[lax.bitwise_xor(place.shard, k), own_spot(self.masks)],
                    self.came[1 + count].at[k - 1],
                    self.sems[:2],
                    self.base + 1 + count * self.rest + k - 1,
                    place.by_shard(k),
                )
                copy.start()
                self.sent.append(copy)
                self.group.append(copy)

        def after_shard():
            total = to_float(self.half[place.shard, own_spot(self.masks)])
            for copy in self.group:
                copy.wait_recv()
            for k in range(1, shards):
                total = total + to_float(self.came[1 + count][k - 1])
            self.back[0] = to_half(total)
            double(0)
            self.write(place.rep, self.back[0])

        def double(stage):
            masks = self.masks + [1]
            size = 1 << stage
            self.fly(
                self.back.at[pl.ds(0, size)],
                self.back.at[pl.ds(size, size)],
                1 + count * self.rest + shards - 1 + stage,
                place.by_rep(masks[stage]),
            )

        def after_double(stage):
            masks = self.masks + [1]
            size = 1 << stage
            self.flight.wait_recv()
            if stage < count:
                double(stage + 1)
            for m in range(size, 2 * size):
                self.write(lax.bitwise_xor(place.rep, offset_of(m, masks)), self.back[m])

        todo.append(after_core)
        for stage in range(count):
            todo.append(lambda stage=stage: after_plane(stage))
        todo.append(after_shard)
        for stage in range(count + 1):
            todo.append(lambda stage=stage: after_double(stage))
        return todo

    def finish(self):
        for copy in self.sent:
            copy.wait_send()


def flights_of(rep_count, shard_count):
    planes = len(plane_masks(rep_count, 0))
    return 1 + planes * (rep_count // 2) + shard_count - 1 + planes + 1


REDUCE_AHEAD = 4


def reduce_body(rep_count, shard_count, units, tensors, *refs):
    planes = len(plane_masks(rep_count, 0))
    sources, outs = refs[:tensors], refs[tensors : 2 * tensors]
    rest = refs[2 * tensors :]
    per_kind = planes + 4
    kinds = [rest[i * per_kind : (i + 1) * per_kind] for i in range(2)]
    send, receive, kept = rest[2 * per_kind :]
    place = Place(rep_count, shard_count)
    place.meet()
    count = flights_of(rep_count, shard_count)
    works = []
    for index, (tensor, pick, writer, kind, slot) in enumerate(units):
        bufs = kinds[kind]
        came = [buf.at[slot] for buf in bufs[1 : 1 + planes + 2]]
        works.append(
            Reduction(
                place,
                index % 2,
                pick(sources[tensor]),
                bufs[0].at[slot],
                came,
                bufs[-1].at[slot],
                (send, receive, kept),
                index * count,
                lambda piece, value, tensor=tensor, writer=writer: writer(
                    outs[tensor], piece, to_float(value)
                ),
            )
        )
    todo = [work.steps() for work in works]
    for work in works[:REDUCE_AHEAD]:
        work.start()
    length = len(todo[0])
    for step in range(len(works) + length - 1):
        for position in range(length - 1, -1, -1):
            index = step - position
            if 0 <= index < len(works):
                todo[index][position]()
                if position == 0 and index + REDUCE_AHEAD < len(works):
                    works[index + REDUCE_AHEAD].start()
    for work in works:
        work.finish()


def reduce_grads(down, up, squares, pack, rep_count, shard_count):
    width = squares[0].shape[1]
    piece = squares[0].shape[0] // (shard_count * rep_count)
    parts = up.shape[1] // width
    lead = (shard_count, rep_count // 2, 2)
    tensors = [down.reshape(lead + (parts, piece, width)), up.reshape(lead + (piece, up.shape[1]))]
    tensors += [g.reshape(lead + (piece, width)) for g in squares]
    pack_rows, pack_width = pack.shape[1] // rep_count, pack.shape[2]
    tensors.append(pack.reshape(lead + (pack_rows, pack_width)))
    outs = [jax.ShapeDtypeStruct((rep_count, parts, piece, width), jnp.float32)]
    outs.append(jax.ShapeDtypeStruct((rep_count, piece, up.shape[1]), jnp.float32))
    outs += [jax.ShapeDtypeStruct((rep_count, piece, width), jnp.float32)] * len(squares)
    outs.append(jax.ShapeDtypeStruct((rep_count, pack_rows, pack_width), jnp.float32))

    def whole_writer(out, at, value):
        out[at] = value

    units = []
    for q in range(parts):

        def part_writer(out, at, value, q=q):
            out[at, q] = value

        units.append((0, lambda ref, q=q: ref.at[:, :, :, q], part_writer, 0, len(units)))
    for q in range(parts):

        def column_writer(out, at, value, q=q):
            out[at, :, q * width : (q + 1) * width] = value

        units.append(
            (
                1,
                lambda ref, q=q: ref.at[:, :, :, :, pl.ds(q * width, width)],
                column_writer,
                0,
                len(units),
            )
        )
    for i in range(len(squares)):
        units.append((2 + i, lambda ref: ref, whole_writer, 0, len(units)))
    plain = len(units)
    units.append((2 + len(squares), lambda ref: ref, whole_writer, 1, 0))
    half = rep_count // 2
    planes = len(plane_masks(rep_count, 0))

    def buffers(count, rows, columns):
        shapes = [(shard_count, half), (shard_count, half)]
        size = half
        for _ in range(planes):
            size //= 2
            shapes.append((size, shard_count))
        shapes += [(shard_count - 1,), (rep_count,)]
        return [pltpu.VMEM((count,) + shape + (rows, columns), jnp.bfloat16) for shape in shapes]

    flights = len(units) * flights_of(rep_count, shard_count)
    anywhere = pl.BlockSpec(memory_space=pl.ANY)
    found = pl.pallas_call(
        lambda *refs: reduce_body(rep_count, shard_count, units, len(tensors), *refs),
        in_specs=[anywhere] * len(tensors),
        out_specs=[pl.BlockSpec(memory_space=pltpu.VMEM)] * len(outs),
        out_shape=outs,
        scratch_shapes=buffers(plain, piece, width)
        + buffers(1, pack_rows, pack_width)
        + [pltpu.SemaphoreType.DMA((flights,))] * 3,
        compiler_params=pltpu.CompilerParams(
            collective_id=1, has_side_effects=True, vmem_limit_bytes=60 * 1024 * 1024
        ),
        cost_estimate=pl.CostEstimate(flops=0, bytes_accessed=200_000_000, transcendentals=0),
        name="reduce_grads",
    )(*tensors)
    rows = rep_count * piece
    return (
        found[0].reshape(rows * parts, width),
        found[1].reshape(rows, up.shape[1]),
        [g.reshape(rows, width) for g in found[2:-1]],
        found[-1].reshape(pack.shape[1], pack_width),
    )


def ssm_kernel_body(coef_ref, rate_ref, out_ref):
    states, lanes = coef_ref.shape
    taps = 64
    count = out_ref.shape[0] // taps
    lag = to_float(lax.broadcasted_iota(jnp.int32, (taps, lanes), 0))

    def step(n, totals):
        rate = rate_ref[pl.ds(n, 1), :]
        factor = coef_ref[pl.ds(n, 1), :]
        block = jnp.exp(-rate * taps)
        decay = jnp.exp(-rate * lag)
        new = []
        for q in range(count):
            new.append(totals[q] + factor * decay)
            factor = factor * block
        return tuple(new)

    zero = jnp.zeros((taps, lanes), jnp.float32)
    totals = lax.fori_loop(0, states, step, (zero,) * count)
    for q in range(count):
        out_ref[q * taps : (q + 1) * taps, :] = totals[q]


def ssm_kernel(coef, rate, length):
    states, channels = coef.shape
    return pl.pallas_call(
        ssm_kernel_body,
        grid=(channels // 128,),
        in_specs=[pl.BlockSpec((states, 128), lambda i: (0, i))] * 2,
        out_specs=pl.BlockSpec((length, 128), lambda i: (0, i)),
        out_shape=jax.ShapeDtypeStruct((length, channels), jnp.float32),
        cost_estimate=pl.CostEstimate(
            flops=2 * states * length * channels,
            bytes_accessed=4 * channels * (2 * states + length),
            transcendentals=states * 64 * channels,
        ),
        name="ssm_kernel",
    )(coef, rate)


def ssm_grad_body(coef_ref, rate_ref, grad_ref, coef_out, rate_out):
    states, lanes = coef_ref.shape
    taps = 64
    count = grad_ref.shape[0] // taps
    lag = to_float(lax.broadcasted_iota(jnp.int32, (taps, lanes), 0))

    def step(n, unused):
        rate = rate_ref[pl.ds(n, 1), :]
        block = jnp.exp(-rate * taps)
        decay = jnp.exp(-rate * lag)
        plain = jnp.zeros((taps, lanes), jnp.float32)
        ramp = jnp.zeros((taps, lanes), jnp.float32)
        for q in range(count - 1, -1, -1):
            grad = grad_ref[q * taps : (q + 1) * taps, :]
            plain = plain * block + grad
            ramp = ramp * block + grad * float(q * taps)
        ramp = ramp + plain * lag
        coef_out[pl.ds(n, 1), :] = jnp.sum(plain * decay, axis=0, keepdims=True)
        rate_out[pl.ds(n, 1), :] = -coef_ref[pl.ds(n, 1), :] * jnp.sum(
            ramp * decay, axis=0, keepdims=True
        )
        return unused

    lax.fori_loop(0, states, step, 0)


def ssm_grad(coef, rate, grad):
    states, channels = coef.shape
    length = grad.shape[0]
    return pl.pallas_call(
        ssm_grad_body,
        grid=(channels // 128,),
        in_specs=[pl.BlockSpec((states, 128), lambda i: (0, i))] * 2
        + [pl.BlockSpec((length, 128), lambda i: (0, i))],
        out_specs=[pl.BlockSpec((states, 128), lambda i: (0, i))] * 2,
        out_shape=[jax.ShapeDtypeStruct((states, channels), jnp.float32)] * 2,
        cost_estimate=pl.CostEstimate(
            flops=6 * states * length * channels,
            bytes_accessed=4 * channels * (4 * states + length),
            transcendentals=states * 64 * channels,
        ),
        name="ssm_grad",
    )(coef, rate, grad)


def wave_tables(rows, period, length):
    freq = lax.broadcasted_iota(jnp.int32, (rows, length), 0)
    time = lax.broadcasted_iota(jnp.int32, (rows, length), 1)
    phase = ((2 * freq + 1) * time) % (2 * period)
    angle = to_float(phase) * (jnp.pi / period)
    return jnp.cos(angle), -jnp.sin(angle)


class Waves:
    def __init__(self, length, short, count):
        self.length, self.short, self.count = length, short, count
        self.half = length + short * count
        top = wave_tables(length, 2 * length, length)
        low = wave_tables(short, 2 * short, short)
        self.long_rows = top
        self.short_rows = low
        parts = []
        for a, b in zip(top, low):
            rows = [jnp.pad(a, ((0, 0), (0, short * count)))]
            for i in range(count):
                rows.append(
                    jnp.pad(b, ((0, 0), (length + i * short, (count - 1 - i) * short)))
                )
            parts.append(jnp.concatenate(rows))
        full = jnp.concatenate(parts)
        self.exact = lax.optimization_barrier(full)
        self.low = lax.optimization_barrier(to_half(full))
        self.gain = jnp.concatenate(
            [
                jnp.full((length, 1), 1.0 / length, jnp.float32),
                jnp.full((short * count, 1), 1.0 / short, jnp.float32),
            ]
        )

    def forward(self, rows):
        return dot_nn(self.low, to_half(rows))

    def back(self, real, imag):
        return dot_tn(self.low, jnp.concatenate([to_half(real), to_half(imag)]))

    def filter(self, taps):
        lags, channels = taps.shape
        first = jnp.pad(taps, ((0, self.length - lags), (0, 0)))
        rows = jnp.concatenate([first] + [taps[: self.short]] * self.count)
        wave = jnp.dot(self.exact, rows, precision=lax.Precision.HIGH)
        return wave[: self.half] * self.gain, wave[self.half :] * self.gain

    def lags(self, real, imag, count):
        real, imag = real * self.gain, imag * self.gain
        channels = real.shape[1]
        length, short = self.length, self.short
        top = jnp.concatenate([real[:length], imag[:length]])
        low = jnp.concatenate(
            [
                jnp.sum(part[length:].reshape(self.count, short, channels), axis=0)
                for part in (real, imag)
            ]
        )
        half, width = self.half, min(count, length)
        table = jnp.concatenate([self.low[:length, :width], self.low[half : half + length, :width]])
        small = jnp.concatenate(
            [
                self.low[length : length + short, length : length + short],
                self.low[half + length : half + length + short, length : length + short],
            ]
        )
        total = dot_tn(table, to_half(top))
        head = total[:short] + dot_tn(small, to_half(low))
        return jnp.concatenate([head, total[short:]]) if count > short else head


def row_stats(values):
    average = jnp.mean(values, axis=-1, keepdims=True)
    centred = values - average
    spread = jnp.mean(centred * centred, axis=-1, keepdims=True)
    scale = lax.rsqrt(spread + EPSILON)
    return centred * scale, scale


def norm_back(error, hat, scale, gain):
    pulled = error * gain
    return scale * (
        pulled
        - jnp.mean(pulled, axis=-1, keepdims=True)
        - hat * jnp.mean(pulled * hat, axis=-1, keepdims=True)
    )


def column_sum(array):
    return jnp.sum(to_float(array), axis=0)


def local(
    tokens,
    ln1_scale,
    ln1_shift,
    w_query,
    b_query,
    w_key,
    b_key,
    w_value,
    b_value,
    shift_taps,
    ssm_coef,
    ssm_rate,
    ssm_skip,
    w_out,
    b_out,
    ln2_scale,
    ln2_shift,
    w_up,
    b_up,
    w_down,
    b_down,
    cotangent,
    piece_slot,
    lengths,
):
    rep_count, shard_count = lax.axis_size("rep"), lax.axis_size("shard")
    slots = rep_count * shard_count
    me = lax.axis_index("rep") * shard_count + lax.axis_index("shard")
    rows, width = tokens.shape
    piece_rows = rows // slots
    taps = shift_taps.shape[1]
    blocks = rows // taps
    owned = ssm_skip.shape[0]
    shorts = lengths.shape[1] - 1
    long_blocks = blocks - shorts
    per_block = slots // blocks

    ids = jnp.arange(slots, dtype=jnp.int32)
    table = piece_slot.reshape(slots, slots)
    target = table // slots
    arrival = jnp.sum(jnp.where(target == me, table % slots, 0), axis=1)
    own_target = jnp.sum(jnp.where(ids[:, None] == me, target, 0), axis=0)
    sizes = lengths[0] // taps
    starts = jnp.cumsum(sizes) - sizes
    first = jnp.sum(jnp.where(sizes == long_blocks, starts, 0))
    block = arrival // per_block
    moved = jnp.where(
        block < first,
        block + long_blocks,
        jnp.where(block < first + long_blocks, block - first, block),
    )
    arrival = moved * per_block + arrival % per_block
    sending = jnp.sum(jnp.where(own_target[None, :] == ids[:, None], ids[None, :], 0), axis=1)
    unpacking = jnp.sum(jnp.where(arrival[None, :] == ids[:, None], ids[None, :], 0), axis=1)

    def deal(array):
        pieces = array.reshape(slots, piece_rows, width)[sending]
        came = lax.all_to_all(pieces, ("rep", "shard"), split_axis=0, concat_axis=0, tiled=True)
        return came[unpacking].reshape(rows, width)

    def give_back(array):
        pieces = array.reshape(slots, piece_rows, width)[arrival]
        came = lax.all_to_all(pieces, ("rep", "shard"), split_axis=0, concat_axis=0, tiled=True)
        return came[own_target].reshape(rows, width)

    balanced = to_float(deal(tokens))

    pack = jnp.concatenate(
        [shift_taps.T, ssm_coef.T, ssm_rate.T]
        + [
            vector.reshape(1, owned)
            for vector in (
                ln1_scale,
                ln1_shift,
                b_query,
                b_key,
                b_value,
                ssm_skip,
                b_out,
                ln2_scale,
                ln2_shift,
                b_down,
            )
        ]
        + [b_up.reshape(-1, owned)]
    )
    (weight_q, weight_k, weight_v, weight_o, weight_up, weight_down), packs = gather_weights(
        [w_query, w_key, w_value, w_out], w_up, w_down, pack, rep_count, shard_count
    )
    tops = 3 * taps + 10
    up_bias = to_float(packs[:, tops:].reshape(1, -1))
    small = to_float(jnp.swapaxes(packs[:, :tops], 0, 1).reshape(tops, width))
    tap_rows, coef_rows, rate_rows = small[:taps], small[taps : 2 * taps], small[2 * taps : 3 * taps]
    (
        gain_one,
        bias_one,
        query_bias,
        key_bias,
        value_bias,
        skip,
        out_bias,
        gain_two,
        bias_two,
        down_bias,
    ) = [small[3 * taps + i][None] for i in range(10)]

    waves = Waves(long_blocks * taps, taps, shorts)
    half = waves.half
    kernel = ssm_kernel(coef_rows, rate_rows, long_blocks * taps)
    ker_re, ker_im = waves.filter(kernel)
    tap_re, tap_im = waves.filter(tap_rows)

    hat_one, scale_one = row_stats(balanced)
    normed = to_half(hat_one * gain_one + bias_one)
    queries = dot_nn(normed, weight_q) + query_bias
    keys = to_half(dot_nn(normed, weight_k) + key_bias)
    values = dot_nn(normed, weight_v) + value_bias
    wave_k = waves.forward(keys)
    key_re, key_im = wave_k[:half], wave_k[half:]
    shifted = waves.back(key_re * tap_re - key_im * tap_im, key_re * tap_im + key_im * tap_re)
    inputs = shifted * values
    wave_u = waves.forward(inputs)
    in_re, in_im = wave_u[:half], wave_u[half:]
    mixed = (
        waves.back(in_re * ker_re - in_im * ker_im, in_re * ker_im + in_im * ker_re)
        + skip * inputs
    )
    gated = to_half(queries * mixed)
    middle = balanced + (dot_nn(gated, weight_o) + out_bias)
    hat_two, scale_two = row_stats(middle)
    normed_two = to_half(hat_two * gain_two + bias_two)

    hidden = dot_nn(normed_two, weight_up) + up_bias
    bent = jnp.tanh(GELU_A * (hidden + GELU_B * hidden * hidden * hidden))
    active = to_half(0.5 * hidden * (1.0 + bent))
    slope = 0.5 * (1.0 + bent) + 0.5 * hidden * (1.0 - bent * bent) * GELU_A * (
        1.0 + 3.0 * GELU_B * hidden * hidden
    )
    branch = dot_nn(active, weight_down)
    result = middle + (branch + down_bias)
    block_output = give_back(to_half(result))

    grad_low = deal(cotangent)
    grad_out = to_float(grad_low)
    part_down = dot_tn(active, grad_low, jnp.bfloat16)
    g_b_down = column_sum(grad_low)
    grad_hidden = to_half(dot_nt(grad_low, weight_down) * slope)
    part_up = dot_tn(normed_two, grad_hidden, jnp.bfloat16)
    g_b_up = column_sum(grad_hidden)
    error = dot_nt(grad_hidden, weight_up)
    g_ln2_scale = jnp.sum(error * hat_two, axis=0)
    g_ln2_shift = jnp.sum(error, axis=0)
    grad_middle = grad_out + norm_back(error, hat_two, scale_two, gain_two)
    grad_branch = to_half(grad_middle)
    part_out = dot_tn(gated, grad_branch, jnp.bfloat16)
    g_b_out = column_sum(grad_branch)
    grad_gated = dot_nt(grad_branch, weight_o)
    grad_query = to_half(grad_gated * mixed)
    part_query = dot_tn(normed, grad_query, jnp.bfloat16)
    grad_mixed = grad_gated * queries
    wave_g = waves.forward(grad_mixed)
    g_re, g_im = wave_g[:half], wave_g[half:]
    grad_inputs = (
        waves.back(g_re * ker_re + g_im * ker_im, g_im * ker_re - g_re * ker_im)
        + skip * grad_mixed
    )
    g_skip = jnp.sum(grad_mixed * inputs, axis=0)
    grad_kernel = waves.lags(
        g_re * in_re + g_im * in_im, g_im * in_re - g_re * in_im, long_blocks * taps
    )
    g_coef, g_rate = ssm_grad(coef_rows, rate_rows, grad_kernel)
    grad_shifted = grad_inputs * values
    grad_value = to_half(grad_inputs * shifted)
    part_value = dot_tn(normed, grad_value, jnp.bfloat16)
    wave_s = waves.forward(grad_shifted)
    s_re, s_im = wave_s[:half], wave_s[half:]
    grad_key = to_half(waves.back(s_re * tap_re + s_im * tap_im, s_im * tap_re - s_re * tap_im))
    g_taps = waves.lags(s_re * key_re + s_im * key_im, s_im * key_re - s_re * key_im, taps)
    part_key = dot_tn(normed, grad_key, jnp.bfloat16)
    grad_normed = (
        dot_nt(grad_query, weight_q) + dot_nt(grad_key, weight_k) + dot_nt(grad_value, weight_v)
    )
    g_ln1_scale = jnp.sum(grad_normed * hat_one, axis=0)
    g_ln1_shift = jnp.sum(grad_normed, axis=0)
    grad_input = grad_middle + norm_back(grad_normed, hat_one, scale_one, gain_one)
    grad_tokens = give_back(to_half(grad_input))

    vectors = [
        g_ln1_scale,
        g_ln1_shift,
        column_sum(grad_query),
        column_sum(grad_key),
        column_sum(grad_value),
        g_skip,
        g_b_out,
        g_ln2_scale,
        g_ln2_shift,
        g_b_down,
    ]
    wide = jnp.concatenate([g_taps, g_coef, g_rate] + [v[None] for v in vectors])
    wide = jnp.swapaxes(wide.reshape(tops, shard_count, owned), 0, 1)
    wide = jnp.concatenate([wide, g_b_up.reshape(shard_count, -1, owned)], axis=1)
    wide = to_half(jnp.pad(wide, ((0, 0), (0, -wide.shape[1] % rep_count), (0, 0))))
    ups = b_up.shape[0] // owned
    grad_w_down, grad_w_up, squares, mine = reduce_grads(
        part_down,
        part_up,
        [part_out, part_query, part_value, part_key],
        wide,
        rep_count,
        shard_count,
    )
    grad_w_out, grad_w_query, grad_w_value, grad_w_key = squares
    vec = [mine[3 * taps + i] for i in range(10)]
    return (
        block_output,
        grad_tokens,
        vec[0],
        vec[1],
        grad_w_query,
        vec[2],
        grad_w_key,
        vec[3],
        grad_w_value,
        vec[4],
        mine[:taps].T,
        mine[taps : 2 * taps].T,
        mine[2 * taps : 3 * taps].T,
        vec[5],
        grad_w_out,
        vec[6],
        vec[7],
        vec[8],
        grad_w_up,
        mine[tops : tops + ups].reshape(-1),
        grad_w_down,
        vec[9],
    )


def solution(mesh):
    both = P(("rep", "shard"), None)
    row, mat = P("shard"), P("shard", None)
    in_specs = (
        (both, row, row, mat, row, mat, row, mat, row, mat, mat, mat, row)
        + (mat, row, row, row, mat, row, mat, row, both, P(), both)
    )
    out_specs = (
        (both, both, row, row, mat, row, mat, row, mat, row, mat, mat, mat, row)
        + (mat, row, row, row, mat, row, mat, row)
    )
    return jax.shard_map(local, mesh=mesh, in_specs=in_specs, out_specs=out_specs, check_vma=False)
```

```python
import jax
import jax.numpy as jnp
from jax import lax
from jax.experimental import pallas as pl
from jax.experimental.pallas import tpu as pltpu
from jax.sharding import PartitionSpec as P

EPSILON = 1e-05
GELU_A = 0.7978845608028654
GELU_B = 0.044715


def to_float(array):
    return array.astype(jnp.float32)


def to_half(array):
    return array.astype(jnp.bfloat16)


def dot_nn(one, two, out=jnp.float32):
    return jnp.dot(one, two, preferred_element_type=jnp.float32).astype(out)


def dot_tn(one, two, out=jnp.float32):
    return lax.dot_general(
        one, two, (((0,), (0,)), ((), ())), preferred_element_type=jnp.float32
    ).astype(out)


def dot_nt(one, two, out=jnp.float32):
    return lax.dot_general(
        one, two, (((1,), (1,)), ((), ())), preferred_element_type=jnp.float32
    ).astype(out)


MESH = pl.DeviceIdType.MESH


class Place:
    def __init__(self, rep_count, shard_count):
        self.rep_count, self.shard_count = rep_count, shard_count
        self.rep, self.shard = lax.axis_index("rep"), lax.axis_index("shard")

    def by_rep(self, mask):
        return (lax.bitwise_xor(self.rep, mask), self.shard)

    def by_shard(self, mask):
        return (self.rep, lax.bitwise_xor(self.shard, mask))

    def bit(self, mask):
        return lax.bitwise_and(lax.div(self.rep, mask), 1)

    def partners(self):
        found, mask = [], 1
        while mask < self.rep_count:
            found.append(self.by_rep(mask))
            mask *= 2
        return found + [self.by_shard(k) for k in range(1, self.shard_count)]

    def meet(self):
        barrier = pltpu.get_barrier_semaphore()
        partners = self.partners()
        for device in partners:
            pl.semaphore_signal(barrier, inc=1, device_id=device, device_id_type=MESH)
        pl.semaphore_wait(barrier, len(partners))

    def meet_all(self):
        barrier = pltpu.get_barrier_semaphore()
        slots = self.rep_count * self.shard_count
        me = self.rep * self.shard_count + self.shard

        def greet(offset, unused):
            device = lax.rem(me + offset, slots)
            pl.semaphore_signal(
                barrier,
                inc=1,
                device_id=(lax.div(device, self.shard_count), lax.rem(device, self.shard_count)),
                device_id_type=MESH,
            )
            return unused

        lax.fori_loop(1, slots, greet, 0)
        pl.semaphore_wait(barrier, slots - 1)


def plane_masks(rep_count, order):
    masks, mask = [], 2
    while mask < rep_count:
        masks.append(mask)
        mask *= 2
    return masks if order == 0 else masks[::-1]


def offset_of(index, masks):
    total = 0
    for i, mask in enumerate(masks):
        if (index >> i) & 1:
            total |= mask
    return total


def remote(source, target, sems, index, device):
    send, receive = sems
    return pltpu.make_async_remote_copy(
        src_ref=source,
        dst_ref=target,
        send_sem=send.at[index],
        recv_sem=receive.at[index],
        device_id=device,
        device_id_type=MESH,
    )


def deal_start(pieces, order, staged, landed, sems, place):
    slots = place.rep_count * place.shard_count
    me = place.rep * place.shard_count + place.shard

    def step(offset, unused):
        device = lax.rem(me + offset, slots)
        chosen = order[device]
        for i, array in enumerate(pieces):
            staged[offset, i] = array[chosen]
        deal_copy(staged, landed, sems, place, offset).start()
        return unused

    lax.fori_loop(1, slots, step, 0)
    for i, array in enumerate(pieces):
        landed[me, i] = array[order[me]]


def deal_copy(staged, landed, sems, place, offset):
    slots = place.rep_count * place.shard_count
    me = place.rep * place.shard_count + place.shard
    device = lax.rem(me + offset, slots)
    return remote(
        staged.at[offset],
        landed.at[me],
        sems,
        offset,
        (lax.div(device, place.shard_count), lax.rem(device, place.shard_count)),
    )


def deal_end(outs, order, staged, landed, sems, place):
    slots = place.rep_count * place.shard_count

    def wait(offset, unused):
        deal_copy(staged, landed, sems, place, offset).wait()
        return unused

    def step(spot, unused):
        chosen = order[spot]
        for i, out in enumerate(outs):
            out[spot] = landed[chosen, i]
        return unused

    lax.fori_loop(1, slots, wait, 0)
    lax.fori_loop(0, slots, step, 0)


def split_half(array):
    high = to_half(array)
    return high, to_half(array - to_float(high))


def dot_fine(one, two):
    (one_high, one_low), (two_high, two_low) = one, two
    total = dot_nn(one_high, two_high) + dot_nn(one_low, two_high)
    return total + dot_nn(one_high, two_low)


def wave_tables(rows, period, length):
    freq = lax.broadcasted_iota(jnp.int32, (rows, length), 0)
    time = lax.broadcasted_iota(jnp.int32, (rows, length), 1)
    phase = lax.rem((2 * freq + 1) * time, 4 * period)
    angle = to_float(phase) * (jnp.pi / (2 * period))
    return jnp.cos(angle), -jnp.sin(angle)


def tile_kernel(coef_ref, rate_ref, out_ref, lanes):
    states, length = coef_ref.shape[0], out_ref.shape[0]
    count = length // 8
    row = to_float(lax.broadcasted_iota(jnp.int32, (8, 128), 0))

    batch = 8

    def step(block, totals):
        first = pl.multiple_of(block * batch, batch)
        rates = rate_ref[pl.ds(first, batch), lanes]
        coefs = coef_ref[pl.ds(first, batch), lanes]
        for n in range(batch):
            rate = jnp.broadcast_to(rates[n : n + 1], (8, 128))
            coef = jnp.broadcast_to(coefs[n : n + 1], (8, 128))
            hop = jnp.exp(rate * -8.0)
            far = jnp.exp(rate * -64.0)
            terms = [coef * jnp.exp(-rate * row)]
            terms.append(terms[0] * hop)
            hop = hop * hop
            terms += [terms[0] * hop, terms[1] * hop]
            hop = hop * hop
            terms += [terms[0] * hop, terms[1] * hop, terms[2] * hop, terms[3] * hop]
            new = []
            for i in range(count):
                if i >= 8:
                    terms[i % 8] = terms[i % 8] * far
                new.append(totals[i] + terms[i % 8])
            totals = new
        return tuple(totals)

    totals = lax.fori_loop(0, states // batch, step, (jnp.zeros((8, 128), jnp.float32),) * count)
    for i in range(count):
        out_ref[8 * i : 8 * i + 8, lanes] = totals[i]


def tile_grads(coef_ref, rate_ref, grad_ref, coef_out, rate_out, lanes):
    states, length = coef_ref.shape[0], grad_ref.shape[0]
    count = length // 8
    row = to_float(lax.broadcasted_iota(jnp.int32, (8, 128), 0))
    batch = 8

    def step(block, unused):
        first = pl.multiple_of(block * batch, batch)
        rates = rate_ref[pl.ds(first, batch), lanes]
        rate = [jnp.broadcast_to(rates[i : i + 1], (8, 128)) for i in range(batch)]
        hop = [jnp.exp(r * -8.0) for r in rate]
        plain = [jnp.zeros((8, 128), jnp.float32) for _ in range(batch)]
        slope = [jnp.zeros((8, 128), jnp.float32) for _ in range(batch)]
        for j in range(count - 1, -1, -1):
            grad = grad_ref[8 * j : 8 * j + 8, lanes]
            for i in range(batch):
                slope[i] = slope[i] * hop[i] + plain[i]
                plain[i] = plain[i] * hop[i] + grad
        ones, twos = [], []
        for i in range(batch):
            start = jnp.exp(-rate[i] * row)
            ones.append(jnp.sum(start * plain[i], axis=0, keepdims=True))
            ramp = start * (8.0 * hop[i] * slope[i] + row * plain[i])
            twos.append(jnp.sum(ramp, axis=0, keepdims=True))
        coef_out[pl.ds(first, batch), lanes] = jnp.concatenate(ones)
        rate_out[pl.ds(first, batch), lanes] = -coef_ref[pl.ds(first, batch), lanes] * (
            jnp.concatenate(twos)
        )
        return unused

    lax.fori_loop(0, states // batch, step, 0)


AHEAD = 6
LAG = 2


def gather_body(rep_count, shard_count, units, shorts, *refs):
    tensors = 1 + max(tensor for tensor, _ in units)
    order, unpack, tokens, cotangent = refs[:4]
    locals_, pack, params = refs[4 : 4 + tensors], refs[4 + tensors], refs[5 + tensors : 8 + tensors]
    rest = refs[8 + tensors :]
    outs, pack_out = rest[:tensors], rest[tensors]
    tokens_out, cotangent_out, kernel_wave, taps_wave, waves, coef_ref, rate_ref = rest[
        tensors + 1 : tensors + 8
    ]
    (held, table, kernel, params_in, staged, landed) = rest[tensors + 8 : tensors + 14]
    send, receive, small_send, small_receive, done, deal_send, deal_receive = rest[tensors + 14 :]
    place = Place(rep_count, shard_count)
    place.meet_all()
    me, shard = place.rep, place.shard
    others = shard_count - 1
    stages = len(plane_masks(rep_count, 0)) + 1
    width = others + stages

    small = []
    owned = params[0].shape[0]
    spot = pl.multiple_of(shard * owned, 8)
    for k in range(1, shard_count):
        for i, source in enumerate((pack,) + tuple(params)):
            target = pack_out.at[shard] if i == 0 else params_in.at[i - 1, shard]
            copy = remote(
                source,
                target,
                (small_send, small_receive),
                (k - 1) * 4 + i,
                place.by_shard(k),
            )
            copy.start()
            small.append(copy)
    own = []
    for i, source in enumerate((pack,) + tuple(params)):
        target = pack_out.at[shard] if i == 0 else params_in.at[i - 1, shard]
        copy = pltpu.make_async_copy(source, target, done.at[tensors + i])
        copy.start()
        own.append(copy)
    deal_start(
        (tokens, cotangent), order, staged, landed, (deal_send, deal_receive), place
    )
    for tensor in range(tensors):
        pltpu.make_async_copy(
            locals_[tensor], outs[tensor].at[shard], done.at[tensor]
        ).start()

    def across(unit):
        tensor, pick = units[unit]
        copies = []
        for k in range(1, shard_count):
            copies.append(
                remote(
                    pick(locals_[tensor].at[me]),
                    held.at[unit, 0, k - 1],
                    (send, receive),
                    unit * width + k - 1,
                    place.by_shard(k),
                )
            )
        return copies

    def doubling(unit, stage):
        masks = plane_masks(rep_count, unit % 2) + [1]
        count = 1 << stage
        return remote(
            held.at[unit, pl.ds(0, count)],
            held.at[unit, pl.ds(count, count)],
            (send, receive),
            unit * width + others + stage,
            place.by_rep(masks[stage]),
        )

    def write(unit, first, count):
        tensor, pick = units[unit]
        masks = plane_masks(rep_count, unit % 2) + [1]
        for m in range(first, first + count):
            piece = lax.bitwise_xor(me, offset_of(m, masks))
            for k in range(1, shard_count):
                pltpu.make_async_copy(
                    held.at[unit, m, k - 1],
                    pick(outs[tensor].at[lax.bitwise_xor(shard, k), piece]),
                    done.at[tensor],
                ).start()

    channels = kernel.shape[1]
    length, taps = kernel.shape[0], params[0].shape[1]
    half = length + shorts * taps
    jobs = []

    def tables():
        for part, (long, short) in enumerate(
            zip(wave_tables(length, length, length), wave_tables(taps, taps, taps))
        ):
            base = part * half
            table[base : base + half, :] = jnp.zeros((half, half), jnp.float32)
            table[base : base + length, 0:length] = long
            for i in range(shorts):
                at = length + i * taps
                table[base + at : base + at + taps, at : at + taps] = short
        waves[...] = to_half(table[...])

    def arrive():
        for copy in small + own:
            copy.wait()

    def arrange(tile):
        lanes = slice(tile * 128, tile * 128 + 128)
        rows = [
            to_float(params_in[i].reshape(channels, taps)[lanes]) for i in range(3)
        ]
        both = jnp.concatenate([rows[1], rows[2]], axis=1).T
        coef_ref[:, lanes] = both[:taps]
        rate_ref[:, lanes] = both[taps:]
        lags = jnp.concatenate([rows[0], rows[0]], axis=1).T
        kernel[0:taps, lanes] = lags[:taps]

    def wave_of(lags, out, fine):
        source = kernel[0:lags, :]
        right = split_half(source) if fine else (to_half(source), None)
        for base in (0, half):
            left = split_half(table[base : base + length, 0:lags])
            if fine:
                top = dot_fine(left, right)
            else:
                top = dot_nn(left[0], right[0]) + dot_nn(left[1], right[0])
            out[base : base + length, :] = top * (1.0 / length)
            left = split_half(table[base + length : base + length + taps, length : length + taps])
            head = [part[:taps] if part is not None else None for part in right]
            if fine:
                low = dot_fine(left, head)
            else:
                low = dot_nn(left[0], head[0]) + dot_nn(left[1], head[0])
            for i in range(shorts):
                at = base + length + i * taps
                out[at : at + taps, :] = low * (1.0 / taps)

    jobs.append(tables)
    jobs.append(arrive)
    for tile in range(channels // 128):
        jobs.append(lambda tile=tile: arrange(tile))
    jobs.append(lambda: wave_of(taps, taps_wave, False))
    for tile in range(channels // 128):
        jobs.append(
            lambda tile=tile: tile_kernel(
                coef_ref, rate_ref, kernel, slice(tile * 128, tile * 128 + 128)
            )
        )
    jobs.append(lambda: wave_of(length, kernel_wave, True))

    flights = {}
    total = len(units)
    for unit in range(min(AHEAD, total)):
        flights[unit, -1] = across(unit)
        for copy in flights[unit, -1]:
            copy.start()
    steps = total + stages * LAG
    per_step = -(-len(jobs) // steps)
    for step in range(steps):
        for stage in range(stages, -1, -1):
            unit = step - stage * LAG
            if not 0 <= unit < total:
                continue
            if stage == 0:
                for copy in flights[unit, -1]:
                    copy.wait_recv()
                if unit + AHEAD < total:
                    flights[unit + AHEAD, -1] = across(unit + AHEAD)
                    for copy in flights[unit + AHEAD, -1]:
                        copy.start()
            else:
                flights[unit, stage - 1].wait_recv()
            if stage < stages:
                flights[unit, stage] = doubling(unit, stage)
                flights[unit, stage].start()
            if stage == 0:
                write(unit, 0, 1)
            else:
                write(unit, 1 << (stage - 1), 1 << (stage - 1))
        for job in jobs[step * per_step : (step + 1) * per_step]:
            job()
    deal_end(
        (tokens_out, cotangent_out), unpack, staged, landed, (deal_send, deal_receive), place
    )
    for unit in range(total):
        for copy in flights[unit, -1]:
            copy.wait_send()
        for stage in range(stages):
            flights[unit, stage].wait_send()
    for tensor in range(tensors):
        pltpu.make_async_copy(outs[tensor], outs[tensor], done.at[tensor]).wait()


def gather_all(order, unpack, tokens, cotangent, squares, up, down, pack, params, counts, shorts):
    rep_count, shard_count = counts
    slots = rep_count * shard_count
    rows, width = squares[0].shape
    piece = rows // rep_count
    parts = up.shape[1] // width
    locals_ = [w.reshape(rep_count, piece, width) for w in squares]
    locals_.append(up.reshape(rep_count, piece, up.shape[1]))
    locals_.append(down.reshape(rep_count, parts, piece, width))
    units = [(i, lambda ref: ref) for i in range(len(squares))]
    for q in range(parts):
        units.append((len(squares), lambda ref, q=q: ref.at[:, pl.ds(q * width, width)]))
    for q in range(parts):
        units.append((len(squares) + 1, lambda ref, q=q: ref.at[q]))
    anywhere = pl.BlockSpec(memory_space=pl.ANY)
    here = pl.BlockSpec(memory_space=pltpu.VMEM)
    scalars = pl.BlockSpec(memory_space=pltpu.SMEM)
    copies = len(units) * (shard_count + len(plane_masks(rep_count, 0)))
    smalls = (shard_count - 1) * 4
    owned, taps = params[0].shape
    channels = owned * shard_count
    half = tokens.shape[0]
    length = half - shorts * taps
    piece_shape = (slots, half // slots, width)
    outs = [jax.ShapeDtypeStruct((shard_count,) + w.shape, w.dtype) for w in locals_ + [pack]]
    spaces = [anywhere] * len(outs) + [here] * 7
    outs += [jax.ShapeDtypeStruct(piece_shape, tokens.dtype)] * 2
    outs += [jax.ShapeDtypeStruct((2 * half, channels), jnp.float32)] * 2
    outs += [jax.ShapeDtypeStruct((2 * half, half), jnp.bfloat16)]
    outs += [jax.ShapeDtypeStruct((taps, channels), jnp.float32)] * 2
    found = pl.pallas_call(
        lambda *refs: gather_body(rep_count, shard_count, units, shorts, *refs),
        in_specs=[scalars] * 2 + [here] * 2 + [anywhere] * (len(locals_) + 4),
        out_specs=spaces,
        out_shape=outs,
        scratch_shapes=[
            pltpu.VMEM((len(units), rep_count, shard_count - 1, piece, width), jnp.bfloat16),
            pltpu.VMEM((2 * half, half), jnp.float32),
            pltpu.VMEM((length, channels), jnp.float32),
            pltpu.VMEM((3, shard_count, owned, taps), jnp.bfloat16),
            pltpu.VMEM((slots, 2) + piece_shape[1:], jnp.bfloat16),
            pltpu.VMEM((slots, 2) + piece_shape[1:], jnp.bfloat16),
            pltpu.SemaphoreType.DMA((copies,)),
            pltpu.SemaphoreType.DMA((copies,)),
            pltpu.SemaphoreType.DMA((smalls,)),
            pltpu.SemaphoreType.DMA((smalls,)),
            pltpu.SemaphoreType.DMA((len(locals_) + 4,)),
            pltpu.SemaphoreType.DMA((slots,)),
            pltpu.SemaphoreType.DMA((slots,)),
        ],
        compiler_params=pltpu.CompilerParams(
            collective_id=0, has_side_effects=True, vmem_limit_bytes=56 * 1024 * 1024
        ),
        cost_estimate=pl.CostEstimate(flops=0, bytes_accessed=200_000_000, transcendentals=0),
        name="gather_all",
    )(
        order,
        unpack,
        tokens.reshape(piece_shape),
        cotangent.reshape(piece_shape),
        *locals_,
        pack,
        *params,
    )
    count = len(squares)
    whole = [w.reshape(shard_count * rows, width) for w in found[:count]]
    whole.append(found[count].reshape(shard_count * rows, up.shape[1]))
    whole.append(found[count + 1].reshape(shard_count * down.shape[0], width))
    packs, balanced, grads = found[count + 2 : count + 5]
    return whole, packs, balanced.reshape(half, width), grads.reshape(half, width), found[count + 5 :]


class Reduction:
    def __init__(self, place, order, source, half, came, back, sems, base, write):
        self.place, self.source, self.half, self.came, self.back = place, source, half, came, back
        self.sems, self.base, self.write = sems, base, write
        self.masks = plane_masks(place.rep_count, order)
        self.flight = None
        self.kept = None
        self.sent = []
        self.rest = place.rep_count // 2

    def start(self):
        place = self.place
        core = place.bit(1)
        self.kept = pltpu.make_async_copy(
            self.source.at[:, :, core], self.half, self.sems[2].at[self.base]
        )
        self.kept.start()
        self.fly(self.source.at[:, :, 1 - core], self.came[0], 0, place.by_rep(1))

    def fly(self, source, target, index, device):
        copy = remote(source, target, self.sems[:2], self.base + index, device)
        copy.start()
        self.sent.append(copy)
        self.flight = copy

    def steps(self):
        place = self.place
        shards = place.shard_count
        count = len(self.masks)
        todo = []

        def after_core():
            self.kept.wait()
            self.flight.wait_recv()
            half, came = self.half, self.came[0]

            def step(i, unused):
                for j in range(self.rest):
                    half[i, j] = to_half(to_float(half[i, j]) + to_float(came[i, j]))
                return unused

            lax.fori_loop(0, shards, step, 0)
            leave(0)

        def index_of(chosen):
            free = [mask for mask in plane_masks(place.rep_count, 0) if mask not in chosen]
            spots = []
            for bits in range(1 << len(free)):
                spot = 0
                for i, mask in enumerate(free):
                    if (bits >> i) & 1:
                        spot += mask // 2
                spots.append(spot)
            return spots

        def own_spot(chosen):
            total = 0
            for mask in chosen:
                total = total + place.bit(mask) * (mask // 2)
            return total

        def leave(stage):
            mask = self.masks[stage]
            chosen = self.masks[: stage + 1]
            base = own_spot(self.masks[:stage]) + (1 - place.bit(mask)) * (mask // 2)
            self.group = []
            for n, spot in enumerate(index_of(chosen)):
                copy = remote(
                    self.half.at[:, base + spot],
                    self.came[1 + stage].at[n],
                    self.sems[:2],
                    self.base + 1 + stage * self.rest + n,
                    place.by_rep(mask),
                )
                copy.start()
                self.sent.append(copy)
                self.group.append(copy)

        def after_plane(stage):
            mask = self.masks[stage]
            chosen = self.masks[: stage + 1]
            base = own_spot(chosen)
            spots = index_of(chosen)
            for copy in self.group:
                copy.wait_recv()
            half, came = self.half, self.came[1 + stage]

            def step(i, unused):
                for n, spot in enumerate(spots):
                    at = base + spot
                    half[i, at] = to_half(to_float(half[i, at]) + to_float(came[n, i]))
                return unused

            lax.fori_loop(0, shards, step, 0)
            if stage + 1 < count:
                leave(stage + 1)
                return
            self.group = []
            for k in range(1, shards):
                copy = remote(
                    self.half.at[lax.bitwise_xor(place.shard, k), own_spot(self.masks)],
                    self.came[1 + count].at[k - 1],
                    self.sems[:2],
                    self.base + 1 + count * self.rest + k - 1,
                    place.by_shard(k),
                )
                copy.start()
                self.sent.append(copy)
                self.group.append(copy)

        def after_shard():
            total = to_float(self.half[place.shard, own_spot(self.masks)])
            for copy in self.group:
                copy.wait_recv()
            for k in range(1, shards):
                total = total + to_float(self.came[1 + count][k - 1])
            self.back[0] = to_half(total)
            double(0)
            self.write(place.rep, self.back[0])

        def double(stage):
            masks = self.masks + [1]
            size = 1 << stage
            self.fly(
                self.back.at[pl.ds(0, size)],
                self.back.at[pl.ds(size, size)],
                1 + count * self.rest + shards - 1 + stage,
                place.by_rep(masks[stage]),
            )

        def after_double(stage):
            masks = self.masks + [1]
            size = 1 << stage
            self.flight.wait_recv()
            if stage < count:
                double(stage + 1)
            for m in range(size, 2 * size):
                self.write(lax.bitwise_xor(place.rep, offset_of(m, masks)), self.back[m])

        todo.append(after_core)
        for stage in range(count):
            todo.append(lambda stage=stage: after_plane(stage))
        todo.append(after_shard)
        for stage in range(count + 1):
            todo.append(lambda stage=stage: after_double(stage))
        return todo

    def finish(self):
        for copy in self.sent:
            copy.wait_send()


def flights_of(rep_count, shard_count):
    planes = len(plane_masks(rep_count, 0))
    return 1 + planes * (rep_count // 2) + shard_count - 1 + planes + 1


REDUCE_AHEAD = 4
REDUCE_LAG = 2


def reduce_body(rep_count, shard_count, units, tensors, kinds_count, *refs):
    planes = len(plane_masks(rep_count, 0))
    order, unpack, grads, coef_ref, rate_ref, kernel_grad, taps_grad = refs[:7]
    sources = list(refs[7 : 6 + tensors])
    outs = refs[6 + tensors : 6 + 2 * tensors]
    grads_out = refs[6 + 2 * tensors]
    rest = refs[7 + 2 * tensors :]
    per_kind = planes + 4
    kinds = [rest[i * per_kind : (i + 1) * per_kind] for i in range(kinds_count)]
    rest = rest[kinds_count * per_kind :]
    made, flat, coef_grad, rate_grad, staged, landed = rest[:6]
    send, receive, kept, deal_send, deal_receive = rest[6:]
    sources.append(made)
    place = Place(rep_count, shard_count)
    place.meet_all()
    count = flights_of(rep_count, shard_count)
    works = []
    for index, (tensor, pick, writer, kind, slot) in enumerate(units):
        bufs = kinds[kind]
        came = [buf.at[slot] for buf in bufs[1 : 1 + planes + 2]]
        works.append(
            Reduction(
                place,
                index % 2,
                pick(sources[tensor]),
                bufs[0].at[slot],
                came,
                bufs[-1].at[slot],
                (send, receive, kept),
                index * count,
                lambda piece, value, tensor=tensor, writer=writer: writer(
                    outs[tensor], piece, to_float(value)
                ),
            )
        )
    taps, channels = taps_grad.shape

    def ssm_job(tile):
        lanes = slice(tile * 128, tile * 128 + 128)
        tile_grads(coef_ref, rate_ref, kernel_grad, coef_grad, rate_grad, lanes)
        both = jnp.concatenate([taps_grad[:, lanes], coef_grad[:, lanes]]).T
        last = jnp.concatenate([rate_grad[:, lanes], rate_grad[:, lanes]]).T
        flat[lanes, :] = jnp.concatenate([both, last[:, :taps]], axis=1)

    def fill_job():
        piece = channels // (shard_count * rep_count)
        for i in range(shard_count * rep_count):
            made[i // rep_count, (i % rep_count) // 2, i % 2] = to_half(
                flat[i * piece : (i + 1) * piece, :]
            )

    jobs = [lambda tile=tile: ssm_job(tile) for tile in range(channels // 128)] + [fill_job]
    todo = [work.steps() for work in works]
    for work in works[:REDUCE_AHEAD]:
        work.start()
    deal_start((grads,), order, staged, landed, (deal_send, deal_receive), place)
    length = len(todo[0])
    for step in range(len(works) + (length - 1) * REDUCE_LAG):
        if step < len(jobs):
            jobs[step]()
        for position in range(length - 1, -1, -1):
            index = step - position * REDUCE_LAG
            if 0 <= index < len(works):
                todo[index][position]()
                if position == 0 and index + REDUCE_AHEAD < len(works):
                    works[index + REDUCE_AHEAD].start()
    deal_end((grads_out,), unpack, staged, landed, (deal_send, deal_receive), place)
    for work in works:
        work.finish()


def reduce_all(order, unpack, grads, rows_in, down, up, squares, pack, counts):
    rep_count, shard_count = counts
    slots = rep_count * shard_count
    width = squares[0].shape[1]
    piece = squares[0].shape[0] // slots
    parts = up.shape[1] // width
    lead = (shard_count, rep_count // 2, 2)
    tensors = [down.reshape(lead + (parts, piece, width)), up.reshape(lead + (piece, up.shape[1]))]
    tensors += [g.reshape(lead + (piece, width)) for g in squares]
    pack_rows, pack_width = pack.shape[1] // rep_count, pack.shape[2]
    tensors.append(pack.reshape(lead + (pack_rows, pack_width)))
    states, channels = rows_in[0].shape
    owned = channels // slots
    outs = [jax.ShapeDtypeStruct((rep_count, parts, piece, width), jnp.float32)]
    outs.append(jax.ShapeDtypeStruct((rep_count, piece, up.shape[1]), jnp.float32))
    outs += [jax.ShapeDtypeStruct((rep_count, piece, width), jnp.float32)] * len(squares)
    outs.append(jax.ShapeDtypeStruct((rep_count, pack_rows, pack_width), jnp.float32))
    outs.append(jax.ShapeDtypeStruct((rep_count, owned, 3 * states), jnp.float32))
    piece_shape = (slots, grads.shape[0] // slots, grads.shape[1])
    outs.append(jax.ShapeDtypeStruct(piece_shape, grads.dtype))

    def whole_writer(out, at, value):
        out[at] = value

    units = []
    for q in range(parts):

        def part_writer(out, at, value, q=q):
            out[at, q] = value

        units.append((0, lambda ref, q=q: ref.at[:, :, :, q], part_writer, 0, len(units)))
    for q in range(parts):

        def column_writer(out, at, value, q=q):
            out[at, :, q * width : (q + 1) * width] = value

        units.append(
            (
                1,
                lambda ref, q=q: ref.at[:, :, :, :, pl.ds(q * width, width)],
                column_writer,
                0,
                len(units),
            )
        )
    for i in range(len(squares)):
        units.append((2 + i, lambda ref: ref, whole_writer, 0, len(units)))
    plain = len(units)
    units.append((2 + len(squares), lambda ref: ref, whole_writer, 1, 0))
    units.append((3 + len(squares), lambda ref: ref, whole_writer, 2, 0))
    half = rep_count // 2
    planes = len(plane_masks(rep_count, 0))

    def buffers(count, rows, columns):
        shapes = [(shard_count, half), (shard_count, half)]
        size = half
        for _ in range(planes):
            size //= 2
            shapes.append((size, shard_count))
        shapes += [(shard_count - 1,), (rep_count,)]
        return [pltpu.VMEM((count,) + shape + (rows, columns), jnp.bfloat16) for shape in shapes]

    flights = len(units) * flights_of(rep_count, shard_count)
    anywhere = pl.BlockSpec(memory_space=pl.ANY)
    here = pl.BlockSpec(memory_space=pltpu.VMEM)
    scalars = pl.BlockSpec(memory_space=pltpu.SMEM)
    found = pl.pallas_call(
        lambda *refs: reduce_body(rep_count, shard_count, units, len(tensors) + 1, 3, *refs),
        in_specs=[scalars] * 2 + [here] * 5 + [anywhere] * len(tensors),
        out_specs=[here] * len(outs),
        out_shape=outs,
        scratch_shapes=buffers(plain, piece, width)
        + buffers(1, pack_rows, pack_width)
        + buffers(1, owned, 3 * states)
        + [
            pltpu.VMEM(lead + (owned, 3 * states), jnp.bfloat16),
            pltpu.VMEM((channels, 3 * states), jnp.float32),
            pltpu.VMEM((states, channels), jnp.float32),
            pltpu.VMEM((states, channels), jnp.float32),
            pltpu.VMEM((slots, 1) + piece_shape[1:], jnp.bfloat16),
            pltpu.VMEM((slots, 1) + piece_shape[1:], jnp.bfloat16),
        ]
        + [pltpu.SemaphoreType.DMA((flights,))] * 3
        + [pltpu.SemaphoreType.DMA((slots,))] * 2,
        compiler_params=pltpu.CompilerParams(
            collective_id=1, has_side_effects=True, vmem_limit_bytes=60 * 1024 * 1024
        ),
        cost_estimate=pl.CostEstimate(flops=0, bytes_accessed=200_000_000, transcendentals=0),
        name="reduce_all",
    )(order, unpack, grads.reshape(piece_shape), *rows_in, *tensors)
    rows = rep_count * piece
    return (
        found[-1].reshape(grads.shape),
        found[0].reshape(rows * parts, width),
        found[1].reshape(rows, up.shape[1]),
        [g.reshape(rows, width) for g in found[2 : 2 + len(squares)]],
        found[-3].reshape(pack.shape[1], pack_width),
        found[-2].reshape(owned * rep_count, 3 * states),
    )


class Waves:
    def __init__(self, table, length, short, count):
        self.low, self.length, self.short, self.count = table, length, short, count
        self.half = length + short * count
        self.gain = jnp.concatenate(
            [
                jnp.full((length, 1), 1.0 / length, jnp.float32),
                jnp.full((short * count, 1), 1.0 / short, jnp.float32),
            ]
        )

    def forward(self, rows):
        return dot_nn(self.low, to_half(rows))

    def back(self, real, imag):
        return dot_tn(self.low, jnp.concatenate([to_half(real), to_half(imag)]))

    def lags(self, real, imag, count):
        real, imag = real * self.gain, imag * self.gain
        channels = real.shape[1]
        length, short = self.length, self.short
        top = jnp.concatenate([real[:length], imag[:length]])
        low = jnp.concatenate(
            [
                jnp.sum(part[length:].reshape(self.count, short, channels), axis=0)
                for part in (real, imag)
            ]
        )
        half, width = self.half, min(count, length)
        table = jnp.concatenate([self.low[:length, :width], self.low[half : half + length, :width]])
        small = jnp.concatenate(
            [
                self.low[length : length + short, length : length + short],
                self.low[half + length : half + length + short, length : length + short],
            ]
        )
        total = dot_tn(table, to_half(top))
        head = total[:short] + dot_tn(small, to_half(low))
        return jnp.concatenate([head, total[short:]]) if count > short else head


def row_stats(values):
    average = jnp.mean(values, axis=-1, keepdims=True)
    centred = values - average
    spread = jnp.mean(centred * centred, axis=-1, keepdims=True)
    scale = lax.rsqrt(spread + EPSILON)
    return centred * scale, scale


def norm_back(error, hat, scale, gain):
    pulled = error * gain
    return scale * (
        pulled
        - jnp.mean(pulled, axis=-1, keepdims=True)
        - hat * jnp.mean(pulled * hat, axis=-1, keepdims=True)
    )


def column_sum(array):
    return jnp.sum(to_float(array), axis=0)


def local(
    tokens,
    ln1_scale,
    ln1_shift,
    w_query,
    b_query,
    w_key,
    b_key,
    w_value,
    b_value,
    shift_taps,
    ssm_coef,
    ssm_rate,
    ssm_skip,
    w_out,
    b_out,
    ln2_scale,
    ln2_shift,
    w_up,
    b_up,
    w_down,
    b_down,
    cotangent,
    piece_slot,
    lengths,
):
    rep_count, shard_count = lax.axis_size("rep"), lax.axis_size("shard")
    slots = rep_count * shard_count
    me = lax.axis_index("rep") * shard_count + lax.axis_index("shard")
    rows, width = tokens.shape
    piece_rows = rows // slots
    taps = shift_taps.shape[1]
    blocks = rows // taps
    owned = ssm_skip.shape[0]
    shorts = lengths.shape[1] - 1
    long_blocks = blocks - shorts
    per_block = slots // blocks

    ids = jnp.arange(slots, dtype=jnp.int32)
    table = piece_slot.reshape(slots, slots)
    target = table // slots
    arrival = jnp.sum(jnp.where(target == me, table % slots, 0), axis=1)
    own_target = jnp.sum(jnp.where(ids[:, None] == me, target, 0), axis=0)
    sizes = lengths[0] // taps
    starts = jnp.cumsum(sizes) - sizes
    first = jnp.sum(jnp.where(sizes == long_blocks, starts, 0))
    block = arrival // per_block
    moved = jnp.where(
        block < first,
        block + long_blocks,
        jnp.where(block < first + long_blocks, block - first, block),
    )
    arrival = moved * per_block + arrival % per_block
    sending = jnp.sum(jnp.where(own_target[None, :] == ids[:, None], ids[None, :], 0), axis=1)
    unpacking = jnp.sum(jnp.where(arrival[None, :] == ids[:, None], ids[None, :], 0), axis=1)

    def give_back(array):
        pieces = array.reshape(slots, piece_rows, width)[arrival]
        came = lax.all_to_all(pieces, ("rep", "shard"), split_axis=0, concat_axis=0, tiled=True)
        return came[own_target].reshape(rows, width)

    pack = jnp.concatenate(
        [
            vector.reshape(1, owned)
            for vector in (
                ln1_scale,
                ln1_shift,
                b_query,
                b_key,
                b_value,
                ssm_skip,
                b_out,
                ln2_scale,
                ln2_shift,
                b_down,
            )
        ]
        + [b_up.reshape(-1, owned)]
    )
    counts = (rep_count, shard_count)
    weights, packs, balanced, grad_low, spectra = gather_all(
        sending,
        unpacking,
        tokens,
        cotangent,
        [w_query, w_key, w_value, w_out],
        w_up,
        w_down,
        pack,
        [shift_taps, ssm_coef, ssm_rate],
        counts,
        shorts,
    )
    weight_q, weight_k, weight_v, weight_o, weight_up, weight_down = weights
    kernel_wave, taps_wave, table, coef_rows, rate_rows = spectra
    balanced = to_float(balanced)
    up_bias = to_float(packs[:, 10:].reshape(1, -1))
    small = to_float(jnp.swapaxes(packs[:, :10], 0, 1).reshape(10, width))
    (
        gain_one,
        bias_one,
        query_bias,
        key_bias,
        value_bias,
        skip,
        out_bias,
        gain_two,
        bias_two,
        down_bias,
    ) = [small[i : i + 1] for i in range(10)]

    waves = Waves(table, long_blocks * taps, taps, shorts)
    half = waves.half
    ker_re, ker_im = kernel_wave[:half], kernel_wave[half:]
    tap_re, tap_im = taps_wave[:half], taps_wave[half:]

    hat_one, scale_one = row_stats(balanced)
    normed = to_half(hat_one * gain_one + bias_one)
    queries = dot_nn(normed, weight_q) + query_bias
    keys = to_half(dot_nn(normed, weight_k) + key_bias)
    values = dot_nn(normed, weight_v) + value_bias
    wave_k = waves.forward(keys)
    key_re, key_im = wave_k[:half], wave_k[half:]
    shifted = waves.back(key_re * tap_re - key_im * tap_im, key_re * tap_im + key_im * tap_re)
    inputs = shifted * values
    wave_u = waves.forward(inputs)
    in_re, in_im = wave_u[:half], wave_u[half:]
    mixed = (
        waves.back(in_re * ker_re - in_im * ker_im, in_re * ker_im + in_im * ker_re)
        + skip * inputs
    )
    gated = to_half(queries * mixed)
    middle = balanced + (dot_nn(gated, weight_o) + out_bias)
    hat_two, scale_two = row_stats(middle)
    normed_two = to_half(hat_two * gain_two + bias_two)

    hidden = dot_nn(normed_two, weight_up) + up_bias
    bent = jnp.tanh(GELU_A * (hidden + GELU_B * hidden * hidden * hidden))
    active = to_half(0.5 * hidden * (1.0 + bent))
    slope = 0.5 * (1.0 + bent) + 0.5 * hidden * (1.0 - bent * bent) * GELU_A * (
        1.0 + 3.0 * GELU_B * hidden * hidden
    )
    branch = dot_nn(active, weight_down)
    result = middle + (branch + down_bias)
    block_output = give_back(to_half(result))

    grad_out = to_float(grad_low)
    part_down = dot_tn(active, grad_low, jnp.bfloat16)
    g_b_down = column_sum(grad_low)
    grad_hidden = to_half(dot_nt(grad_low, weight_down) * slope)
    part_up = dot_tn(normed_two, grad_hidden, jnp.bfloat16)
    g_b_up = column_sum(grad_hidden)
    error = dot_nt(grad_hidden, weight_up)
    g_ln2_scale = jnp.sum(error * hat_two, axis=0)
    g_ln2_shift = jnp.sum(error, axis=0)
    grad_middle = grad_out + norm_back(error, hat_two, scale_two, gain_two)
    grad_branch = to_half(grad_middle)
    part_out = dot_tn(gated, grad_branch, jnp.bfloat16)
    g_b_out = column_sum(grad_branch)
    grad_gated = dot_nt(grad_branch, weight_o)
    grad_query = to_half(grad_gated * mixed)
    part_query = dot_tn(normed, grad_query, jnp.bfloat16)
    grad_mixed = grad_gated * queries
    wave_g = waves.forward(grad_mixed)
    g_re, g_im = wave_g[:half], wave_g[half:]
    grad_inputs = (
        waves.back(g_re * ker_re + g_im * ker_im, g_im * ker_re - g_re * ker_im)
        + skip * grad_mixed
    )
    g_skip = jnp.sum(grad_mixed * inputs, axis=0)
    grad_kernel = waves.lags(
        g_re * in_re + g_im * in_im, g_im * in_re - g_re * in_im, long_blocks * taps
    )
    grad_shifted = grad_inputs * values
    grad_value = to_half(grad_inputs * shifted)
    part_value = dot_tn(normed, grad_value, jnp.bfloat16)
    wave_s = waves.forward(grad_shifted)
    s_re, s_im = wave_s[:half], wave_s[half:]
    grad_key = to_half(waves.back(s_re * tap_re + s_im * tap_im, s_im * tap_re - s_re * tap_im))
    g_taps = waves.lags(s_re * key_re + s_im * key_im, s_im * key_re - s_re * key_im, taps)
    part_key = dot_tn(normed, grad_key, jnp.bfloat16)
    grad_normed = (
        dot_nt(grad_query, weight_q) + dot_nt(grad_key, weight_k) + dot_nt(grad_value, weight_v)
    )
    g_ln1_scale = jnp.sum(grad_normed * hat_one, axis=0)
    g_ln1_shift = jnp.sum(grad_normed, axis=0)
    grad_input = grad_middle + norm_back(grad_normed, hat_one, scale_one, gain_one)

    vectors = [
        g_ln1_scale,
        g_ln1_shift,
        column_sum(grad_query),
        column_sum(grad_key),
        column_sum(grad_value),
        g_skip,
        g_b_out,
        g_ln2_scale,
        g_ln2_shift,
        g_b_down,
    ]
    wide = jnp.concatenate([v[None] for v in vectors])
    wide = jnp.swapaxes(wide.reshape(10, shard_count, owned), 0, 1)
    wide = jnp.concatenate([wide, g_b_up.reshape(shard_count, -1, owned)], axis=1)
    wide = to_half(jnp.pad(wide, ((0, 0), (0, -wide.shape[1] % rep_count), (0, 0))))
    ups = b_up.shape[0] // owned
    grad_tokens, grad_w_down, grad_w_up, squares, mine, ssm = reduce_all(
        arrival,
        own_target,
        to_half(grad_input),
        [coef_rows, rate_rows, grad_kernel, g_taps],
        part_down,
        part_up,
        [part_out, part_query, part_value, part_key],
        wide,
        counts,
    )
    grad_w_out, grad_w_query, grad_w_value, grad_w_key = squares
    vec = [mine[i] for i in range(10)]
    return (
        block_output,
        grad_tokens,
        vec[0],
        vec[1],
        grad_w_query,
        vec[2],
        grad_w_key,
        vec[3],
        grad_w_value,
        vec[4],
        ssm[:, :taps],
        ssm[:, taps : 2 * taps],
        ssm[:, 2 * taps :],
        vec[5],
        grad_w_out,
        vec[6],
        vec[7],
        vec[8],
        grad_w_up,
        mine[10 : 10 + ups].reshape(-1),
        grad_w_down,
        vec[9],
    )


def solution(mesh):
    both = P(("rep", "shard"), None)
    row, mat = P("shard"), P("shard", None)
    in_specs = (
        (both, row, row, mat, row, mat, row, mat, row, mat, mat, mat, row)
        + (mat, row, row, row, mat, row, mat, row, both, P(), both)
    )
    out_specs = (
        (both, both, row, row, mat, row, mat, row, mat, row, mat, mat, mat, row)
        + (mat, row, row, row, mat, row, mat, row)
    )
    return jax.shard_map(local, mesh=mesh, in_specs=in_specs, out_specs=out_specs, check_vma=False)
```

```python
import jax
import jax.numpy as jnp
from jax import lax
from jax.experimental import pallas as pl
from jax.experimental.pallas import tpu as pltpu
from jax.sharding import PartitionSpec as P

EPSILON = 1e-05
GELU_A = 0.7978845608028654
GELU_B = 0.044715


def to_float(array):
    return array.astype(jnp.float32)


def to_half(array):
    return array.astype(jnp.bfloat16)


def dot_nn(one, two, out=jnp.float32):
    return jnp.dot(one, two, preferred_element_type=jnp.float32).astype(out)


def dot_tn(one, two, out=jnp.float32):
    return lax.dot_general(
        one, two, (((0,), (0,)), ((), ())), preferred_element_type=jnp.float32
    ).astype(out)


def dot_nt(one, two, out=jnp.float32):
    return lax.dot_general(
        one, two, (((1,), (1,)), ((), ())), preferred_element_type=jnp.float32
    ).astype(out)


MESH = pl.DeviceIdType.MESH


class Place:
    def __init__(self, rep_count, shard_count):
        self.rep_count, self.shard_count = rep_count, shard_count
        self.rep, self.shard = lax.axis_index("rep"), lax.axis_index("shard")

    def by_rep(self, mask):
        return (lax.bitwise_xor(self.rep, mask), self.shard)

    def by_shard(self, mask):
        return (self.rep, lax.bitwise_xor(self.shard, mask))

    def bit(self, mask):
        return lax.bitwise_and(lax.div(self.rep, mask), 1)

    def partners(self):
        found, mask = [], 1
        while mask < self.rep_count:
            found.append(self.by_rep(mask))
            mask *= 2
        return found + [self.by_shard(k) for k in range(1, self.shard_count)]

    def meet(self):
        barrier = pltpu.get_barrier_semaphore()
        partners = self.partners()
        for device in partners:
            pl.semaphore_signal(barrier, inc=1, device_id=device, device_id_type=MESH)
        pl.semaphore_wait(barrier, len(partners))

    def meet_all(self):
        barrier = pltpu.get_barrier_semaphore()
        slots = self.rep_count * self.shard_count
        me = self.rep * self.shard_count + self.shard

        def greet(offset, unused):
            device = lax.rem(me + offset, slots)
            pl.semaphore_signal(
                barrier,
                inc=1,
                device_id=(lax.div(device, self.shard_count), lax.rem(device, self.shard_count)),
                device_id_type=MESH,
            )
            return unused

        lax.fori_loop(1, slots, greet, 0)
        pl.semaphore_wait(barrier, slots - 1)


def plane_masks(rep_count, order):
    masks, mask = [], 2
    while mask < rep_count:
        masks.append(mask)
        mask *= 2
    return masks if order == 0 else masks[::-1]


def offset_of(index, masks):
    total = 0
    for i, mask in enumerate(masks):
        if (index >> i) & 1:
            total |= mask
    return total


def remote(source, target, sems, index, device):
    send, receive = sems
    return pltpu.make_async_remote_copy(
        src_ref=source,
        dst_ref=target,
        send_sem=send.at[index],
        recv_sem=receive.at[index],
        device_id=device,
        device_id_type=MESH,
    )


def deal_start(pieces, order, staged, landed, sems, place):
    slots = place.rep_count * place.shard_count
    me = place.rep * place.shard_count + place.shard

    def step(offset, unused):
        device = lax.rem(me + offset, slots)
        chosen = order[device]
        for i, array in enumerate(pieces):
            staged[offset, i] = array[chosen]
        deal_copy(staged, landed, sems, place, offset).start()
        return unused

    lax.fori_loop(1, slots, step, 0)
    for i, array in enumerate(pieces):
        landed[me, i] = array[order[me]]


def deal_copy(staged, landed, sems, place, offset):
    slots = place.rep_count * place.shard_count
    me = place.rep * place.shard_count + place.shard
    device = lax.rem(me + offset, slots)
    return remote(
        staged.at[offset],
        landed.at[me],
        sems,
        offset,
        (lax.div(device, place.shard_count), lax.rem(device, place.shard_count)),
    )


def deal_end(outs, order, staged, landed, sems, place):
    slots = place.rep_count * place.shard_count

    def wait(offset, unused):
        deal_copy(staged, landed, sems, place, offset).wait()
        return unused

    def step(spot, unused):
        chosen = order[spot]
        for i, out in enumerate(outs):
            out[spot] = landed[chosen, i]
        return unused

    lax.fori_loop(1, slots, wait, 0)
    lax.fori_loop(0, slots, step, 0)


def split_half(array):
    high = to_half(array)
    return high, to_half(array - to_float(high))


def dot_fine(one, two):
    (one_high, one_low), (two_high, two_low) = one, two
    total = dot_nn(one_high, two_high) + dot_nn(one_low, two_high)
    return total + dot_nn(one_high, two_low)


def wave_tables(rows, period, length):
    freq = lax.broadcasted_iota(jnp.int32, (rows, length), 0)
    time = lax.broadcasted_iota(jnp.int32, (rows, length), 1)
    phase = lax.rem((2 * freq + 1) * time, 4 * period)
    angle = to_float(phase) * (jnp.pi / (2 * period))
    return jnp.cos(angle), -jnp.sin(angle)


def tile_kernel(coef_ref, rate_ref, out_ref, lanes):
    states, length = coef_ref.shape[0], out_ref.shape[0]
    count = length // 8
    row = to_float(lax.broadcasted_iota(jnp.int32, (8, 128), 0))

    batch = 8

    def step(block, totals):
        first = pl.multiple_of(block * batch, batch)
        rates = rate_ref[pl.ds(first, batch), lanes]
        coefs = coef_ref[pl.ds(first, batch), lanes]
        for n in range(batch):
            rate = jnp.broadcast_to(rates[n : n + 1], (8, 128))
            coef = jnp.broadcast_to(coefs[n : n + 1], (8, 128))
            hop = jnp.exp(rate * -8.0)
            far = jnp.exp(rate * -64.0)
            terms = [coef * jnp.exp(-rate * row)]
            terms.append(terms[0] * hop)
            hop = hop * hop
            terms += [terms[0] * hop, terms[1] * hop]
            hop = hop * hop
            terms += [terms[0] * hop, terms[1] * hop, terms[2] * hop, terms[3] * hop]
            new = []
            for i in range(count):
                if i >= 8:
                    terms[i % 8] = terms[i % 8] * far
                new.append(totals[i] + terms[i % 8])
            totals = new
        return tuple(totals)

    totals = lax.fori_loop(0, states // batch, step, (jnp.zeros((8, 128), jnp.float32),) * count)
    for i in range(count):
        out_ref[8 * i : 8 * i + 8, lanes] = totals[i]


def tile_grads(coef_ref, rate_ref, grad_ref, coef_out, rate_out, lanes):
    states, length = coef_ref.shape[0], grad_ref.shape[0]
    count = length // 8
    row = to_float(lax.broadcasted_iota(jnp.int32, (8, 128), 0))
    batch = 8

    def step(block, unused):
        first = pl.multiple_of(block * batch, batch)
        rates = rate_ref[pl.ds(first, batch), lanes]
        rate = [jnp.broadcast_to(rates[i : i + 1], (8, 128)) for i in range(batch)]
        hop = [jnp.exp(r * -8.0) for r in rate]
        plain = [jnp.zeros((8, 128), jnp.float32) for _ in range(batch)]
        slope = [jnp.zeros((8, 128), jnp.float32) for _ in range(batch)]
        for j in range(count - 1, -1, -1):
            grad = grad_ref[8 * j : 8 * j + 8, lanes]
            for i in range(batch):
                slope[i] = slope[i] * hop[i] + plain[i]
                plain[i] = plain[i] * hop[i] + grad
        ones, twos = [], []
        for i in range(batch):
            start = jnp.exp(-rate[i] * row)
            ones.append(jnp.sum(start * plain[i], axis=0, keepdims=True))
            ramp = start * (8.0 * hop[i] * slope[i] + row * plain[i])
            twos.append(jnp.sum(ramp, axis=0, keepdims=True))
        coef_out[pl.ds(first, batch), lanes] = jnp.concatenate(ones)
        rate_out[pl.ds(first, batch), lanes] = -coef_ref[pl.ds(first, batch), lanes] * (
            jnp.concatenate(twos)
        )
        return unused

    lax.fori_loop(0, states // batch, step, 0)


AHEAD = 6
LAG = 2


def gather_body(rep_count, shard_count, units, shorts, *refs):
    tensors = 1 + max(tensor for tensor, _ in units)
    order, unpack, tokens, cotangent = refs[:4]
    locals_, pack, params = refs[4 : 4 + tensors], refs[4 + tensors], refs[5 + tensors : 8 + tensors]
    rest = refs[8 + tensors :]
    outs, pack_out = rest[:tensors], rest[tensors]
    tokens_out, cotangent_out, kernel_wave, taps_wave, waves, waves_t, coef_ref, rate_ref = rest[
        tensors + 1 : tensors + 9
    ]
    (held, table, kernel, params_in, staged, landed) = rest[tensors + 9 : tensors + 15]
    send, receive, small_send, small_receive, done, deal_send, deal_receive = rest[tensors + 15 :]
    place = Place(rep_count, shard_count)
    place.meet_all()
    me, shard = place.rep, place.shard
    others = shard_count - 1
    stages = len(plane_masks(rep_count, 0)) + 1
    width = others + stages

    small = []
    owned = params[0].shape[0]
    spot = pl.multiple_of(shard * owned, 8)
    for k in range(1, shard_count):
        for i, source in enumerate((pack,) + tuple(params)):
            target = pack_out.at[shard] if i == 0 else params_in.at[i - 1, shard]
            copy = remote(
                source,
                target,
                (small_send, small_receive),
                (k - 1) * 4 + i,
                place.by_shard(k),
            )
            copy.start()
            small.append(copy)
    own = []
    for i, source in enumerate((pack,) + tuple(params)):
        target = pack_out.at[shard] if i == 0 else params_in.at[i - 1, shard]
        copy = pltpu.make_async_copy(source, target, done.at[tensors + i])
        copy.start()
        own.append(copy)
    deal_start(
        (tokens, cotangent), order, staged, landed, (deal_send, deal_receive), place
    )
    for tensor in range(tensors):
        pltpu.make_async_copy(
            locals_[tensor], outs[tensor].at[shard], done.at[tensor]
        ).start()

    def across(unit):
        tensor, pick = units[unit]
        copies = []
        for k in range(1, shard_count):
            copies.append(
                remote(
                    pick(locals_[tensor].at[me]),
                    held.at[unit, 0, k - 1],
                    (send, receive),
                    unit * width + k - 1,
                    place.by_shard(k),
                )
            )
        return copies

    def doubling(unit, stage):
        masks = plane_masks(rep_count, unit % 2) + [1]
        count = 1 << stage
        return remote(
            held.at[unit, pl.ds(0, count)],
            held.at[unit, pl.ds(count, count)],
            (send, receive),
            unit * width + others + stage,
            place.by_rep(masks[stage]),
        )

    def write(unit, first, count):
        tensor, pick = units[unit]
        masks = plane_masks(rep_count, unit % 2) + [1]
        for m in range(first, first + count):
            piece = lax.bitwise_xor(me, offset_of(m, masks))
            for k in range(1, shard_count):
                pltpu.make_async_copy(
                    held.at[unit, m, k - 1],
                    pick(outs[tensor].at[lax.bitwise_xor(shard, k), piece]),
                    done.at[tensor],
                ).start()

    channels = kernel.shape[1]
    length, taps = kernel.shape[0], params[0].shape[1]
    half = length + shorts * taps
    jobs = []

    def tables():
        for part, (long, short) in enumerate(
            zip(wave_tables(length, length, length), wave_tables(taps, taps, taps))
        ):
            base = part * half
            table[base : base + half, :] = jnp.zeros((half, half), jnp.float32)
            table[base : base + length, 0:length] = long
            for i in range(shorts):
                at = length + i * taps
                table[base + at : base + at + taps, at : at + taps] = short
        waves[...] = to_half(table[...])
        waves_t[...] = to_half(table[...].T)

    def arrive():
        for copy in small + own:
            copy.wait()

    def arrange(tile):
        lanes = slice(tile * 128, tile * 128 + 128)
        rows = [
            to_float(params_in[i].reshape(channels, taps)[lanes]) for i in range(3)
        ]
        both = jnp.concatenate([rows[1], rows[2]], axis=1).T
        coef_ref[:, lanes] = both[:taps]
        rate_ref[:, lanes] = both[taps:]
        lags = jnp.concatenate([rows[0], rows[0]], axis=1).T
        kernel[0:taps, lanes] = lags[:taps]

    def wave_of(lags, out, fine):
        source = kernel[0:lags, :]
        right = split_half(source) if fine else (to_half(source), None)
        for base in (0, half):
            left = split_half(table[base : base + length, 0:lags])
            if fine:
                top = dot_fine(left, right)
            else:
                top = dot_nn(left[0], right[0]) + dot_nn(left[1], right[0])
            out[base : base + length, :] = to_half(top * (1.0 / length))
            left = split_half(table[base + length : base + length + taps, length : length + taps])
            head = [part[:taps] if part is not None else None for part in right]
            if fine:
                low = dot_fine(left, head)
            else:
                low = dot_nn(left[0], head[0]) + dot_nn(left[1], head[0])
            for i in range(shorts):
                at = base + length + i * taps
                out[at : at + taps, :] = to_half(low * (1.0 / taps))

    jobs.append(tables)
    jobs.append(arrive)
    for tile in range(channels // 128):
        jobs.append(lambda tile=tile: arrange(tile))
    jobs.append(lambda: wave_of(taps, taps_wave, False))
    for tile in range(channels // 128):
        jobs.append(
            lambda tile=tile: tile_kernel(
                coef_ref, rate_ref, kernel, slice(tile * 128, tile * 128 + 128)
            )
        )
    jobs.append(lambda: wave_of(length, kernel_wave, True))

    flights = {}
    total = len(units)
    for unit in range(min(AHEAD, total)):
        flights[unit, -1] = across(unit)
        for copy in flights[unit, -1]:
            copy.start()
    steps = total + stages * LAG
    per_step = -(-len(jobs) // steps)
    for step in range(steps):
        for stage in range(stages, -1, -1):
            unit = step - stage * LAG
            if not 0 <= unit < total:
                continue
            if stage == 0:
                for copy in flights[unit, -1]:
                    copy.wait_recv()
                if unit + AHEAD < total:
                    flights[unit + AHEAD, -1] = across(unit + AHEAD)
                    for copy in flights[unit + AHEAD, -1]:
                        copy.start()
            else:
                flights[unit, stage - 1].wait_recv()
            if stage < stages:
                flights[unit, stage] = doubling(unit, stage)
                flights[unit, stage].start()
            if stage == 0:
                write(unit, 0, 1)
            else:
                write(unit, 1 << (stage - 1), 1 << (stage - 1))
        for job in jobs[step * per_step : (step + 1) * per_step]:
            job()
    deal_end(
        (tokens_out, cotangent_out), unpack, staged, landed, (deal_send, deal_receive), place
    )
    for unit in range(total):
        for copy in flights[unit, -1]:
            copy.wait_send()
        for stage in range(stages):
            flights[unit, stage].wait_send()
    for tensor in range(tensors):
        pltpu.make_async_copy(outs[tensor], outs[tensor], done.at[tensor]).wait()


def gather_all(order, unpack, tokens, cotangent, squares, up, down, pack, params, counts, shorts):
    rep_count, shard_count = counts
    slots = rep_count * shard_count
    rows, width = squares[0].shape
    piece = rows // rep_count
    parts = up.shape[1] // width
    locals_ = [w.reshape(rep_count, piece, width) for w in squares]
    locals_.append(up.reshape(rep_count, piece, up.shape[1]))
    locals_.append(down.reshape(rep_count, parts, piece, width))
    units = [(i, lambda ref: ref) for i in range(len(squares))]
    for q in range(parts):
        units.append((len(squares), lambda ref, q=q: ref.at[:, pl.ds(q * width, width)]))
    for q in range(parts):
        units.append((len(squares) + 1, lambda ref, q=q: ref.at[q]))
    anywhere = pl.BlockSpec(memory_space=pl.ANY)
    here = pl.BlockSpec(memory_space=pltpu.VMEM)
    scalars = pl.BlockSpec(memory_space=pltpu.SMEM)
    copies = len(units) * (shard_count + len(plane_masks(rep_count, 0)))
    smalls = (shard_count - 1) * 4
    owned, taps = params[0].shape
    channels = owned * shard_count
    half = tokens.shape[0]
    length = half - shorts * taps
    piece_shape = (slots, half // slots, width)
    outs = [jax.ShapeDtypeStruct((shard_count,) + w.shape, w.dtype) for w in locals_ + [pack]]
    spaces = [anywhere] * len(outs) + [here] * 8
    outs += [jax.ShapeDtypeStruct(piece_shape, tokens.dtype)] * 2
    outs += [jax.ShapeDtypeStruct((2 * half, channels), jnp.bfloat16)] * 2
    outs += [jax.ShapeDtypeStruct((2 * half, half), jnp.bfloat16)]
    outs += [jax.ShapeDtypeStruct((half, 2 * half), jnp.bfloat16)]
    outs += [jax.ShapeDtypeStruct((taps, channels), jnp.float32)] * 2
    found = pl.pallas_call(
        lambda *refs: gather_body(rep_count, shard_count, units, shorts, *refs),
        in_specs=[scalars] * 2 + [here] * 2 + [anywhere] * (len(locals_) + 4),
        out_specs=spaces,
        out_shape=outs,
        scratch_shapes=[
            pltpu.VMEM((len(units), rep_count, shard_count - 1, piece, width), jnp.bfloat16),
            pltpu.VMEM((2 * half, half), jnp.float32),
            pltpu.VMEM((length, channels), jnp.float32),
            pltpu.VMEM((3, shard_count, owned, taps), jnp.bfloat16),
            pltpu.VMEM((slots, 2) + piece_shape[1:], jnp.bfloat16),
            pltpu.VMEM((slots, 2) + piece_shape[1:], jnp.bfloat16),
            pltpu.SemaphoreType.DMA((copies,)),
            pltpu.SemaphoreType.DMA((copies,)),
            pltpu.SemaphoreType.DMA((smalls,)),
            pltpu.SemaphoreType.DMA((smalls,)),
            pltpu.SemaphoreType.DMA((len(locals_) + 4,)),
            pltpu.SemaphoreType.DMA((slots,)),
            pltpu.SemaphoreType.DMA((slots,)),
        ],
        compiler_params=pltpu.CompilerParams(
            collective_id=0, has_side_effects=True, vmem_limit_bytes=56 * 1024 * 1024
        ),
        cost_estimate=pl.CostEstimate(flops=0, bytes_accessed=200_000_000, transcendentals=0),
        name="gather_all",
    )(
        order,
        unpack,
        tokens.reshape(piece_shape),
        cotangent.reshape(piece_shape),
        *locals_,
        pack,
        *params,
    )
    count = len(squares)
    whole = [w.reshape(shard_count * rows, width) for w in found[:count]]
    whole.append(found[count].reshape(shard_count * rows, up.shape[1]))
    whole.append(found[count + 1].reshape(shard_count * down.shape[0], width))
    packs, balanced, grads = found[count + 2 : count + 5]
    return whole, packs, balanced.reshape(half, width), grads.reshape(half, width), found[count + 5 :]


class Reduction:
    def __init__(self, place, order, source, half, came, back, sems, base, write):
        self.place, self.source, self.half, self.came, self.back = place, source, half, came, back
        self.sems, self.base, self.write = sems, base, write
        self.masks = plane_masks(place.rep_count, order)
        self.flight = None
        self.kept = None
        self.sent = []
        self.rest = place.rep_count // 2

    def start(self):
        place = self.place
        core = place.bit(1)
        if self.half is None:
            self.half = self.source.at[:, :, core]
        else:
            self.kept = pltpu.make_async_copy(
                self.source.at[:, :, core], self.half, self.sems[2].at[self.base]
            )
            self.kept.start()
        self.fly(self.source.at[:, :, 1 - core], self.came[0], 0, place.by_rep(1))

    def fly(self, source, target, index, device):
        copy = remote(source, target, self.sems[:2], self.base + index, device)
        copy.start()
        self.sent.append(copy)
        self.flight = copy

    def steps(self):
        place = self.place
        shards = place.shard_count
        count = len(self.masks)
        todo = []

        def after_core():
            if self.kept is not None:
                self.kept.wait()
            self.flight.wait_recv()
            half, came = self.half, self.came[0]

            def step(i, unused):
                for j in range(self.rest):
                    half[i, j] = to_half(to_float(half[i, j]) + to_float(came[i, j]))
                return unused

            lax.fori_loop(0, shards, step, 0)
            leave(0)

        def index_of(chosen):
            free = [mask for mask in plane_masks(place.rep_count, 0) if mask not in chosen]
            spots = []
            for bits in range(1 << len(free)):
                spot = 0
                for i, mask in enumerate(free):
                    if (bits >> i) & 1:
                        spot += mask // 2
                spots.append(spot)
            return spots

        def own_spot(chosen):
            total = 0
            for mask in chosen:
                total = total + place.bit(mask) * (mask // 2)
            return total

        def leave(stage):
            mask = self.masks[stage]
            chosen = self.masks[: stage + 1]
            base = own_spot(self.masks[:stage]) + (1 - place.bit(mask)) * (mask // 2)
            self.group = []
            for n, spot in enumerate(index_of(chosen)):
                copy = remote(
                    self.half.at[:, base + spot],
                    self.came[1 + stage].at[n],
                    self.sems[:2],
                    self.base + 1 + stage * self.rest + n,
                    place.by_rep(mask),
                )
                copy.start()
                self.sent.append(copy)
                self.group.append(copy)

        def after_plane(stage):
            mask = self.masks[stage]
            chosen = self.masks[: stage + 1]
            base = own_spot(chosen)
            spots = index_of(chosen)
            for copy in self.group:
                copy.wait_recv()
            half, came = self.half, self.came[1 + stage]

            def step(i, unused):
                for n, spot in enumerate(spots):
                    at = base + spot
                    half[i, at] = to_half(to_float(half[i, at]) + to_float(came[n, i]))
                return unused

            lax.fori_loop(0, shards, step, 0)
            if stage + 1 < count:
                leave(stage + 1)
                return
            self.group = []
            for k in range(1, shards):
                copy = remote(
                    self.half.at[lax.bitwise_xor(place.shard, k), own_spot(self.masks)],
                    self.came[1 + count].at[k - 1],
                    self.sems[:2],
                    self.base + 1 + count * self.rest + k - 1,
                    place.by_shard(k),
                )
                copy.start()
                self.sent.append(copy)
                self.group.append(copy)

        def after_shard():
            total = to_float(self.half[place.shard, own_spot(self.masks)])
            for copy in self.group:
                copy.wait_recv()
            for k in range(1, shards):
                total = total + to_float(self.came[1 + count][k - 1])
            self.back[0] = to_half(total)
            double(0)
            self.write(place.rep, self.back.at[0])

        def double(stage):
            masks = self.masks + [1]
            size = 1 << stage
            self.fly(
                self.back.at[pl.ds(0, size)],
                self.back.at[pl.ds(size, size)],
                1 + count * self.rest + shards - 1 + stage,
                place.by_rep(masks[stage]),
            )

        def after_double(stage):
            masks = self.masks + [1]
            size = 1 << stage
            self.flight.wait_recv()
            if stage < count:
                double(stage + 1)
            for m in range(size, 2 * size):
                self.write(lax.bitwise_xor(place.rep, offset_of(m, masks)), self.back.at[m])

        todo.append(after_core)
        for stage in range(count):
            todo.append(lambda stage=stage: after_plane(stage))
        todo.append(after_shard)
        for stage in range(count + 1):
            todo.append(lambda stage=stage: after_double(stage))
        return todo

    def finish(self):
        for copy in self.sent:
            copy.wait_send()


def flights_of(rep_count, shard_count):
    planes = len(plane_masks(rep_count, 0))
    return 1 + planes * (rep_count // 2) + shard_count - 1 + planes + 1


REDUCE_AHEAD = 4
REDUCE_LAG = 2


def loads_of(pairs, sems):
    copies = []
    for i, (source, target) in enumerate(pairs):
        copy = pltpu.make_async_copy(source, target, sems.at[i])
        copy.start()
        copies.append(copy)
    return copies


VECTORS = 16


def sum_everywhere(place, totals, came, sems, base):
    devices, mask = [], 1
    while mask < place.rep_count:
        devices.append(place.by_rep(mask))
        mask *= 2
    mask = 1
    while mask < place.shard_count:
        devices.append(place.by_shard(mask))
        mask *= 2
    flights = []

    def send(stage):
        copy = remote(totals.at[stage], came.at[stage], sems, base + stage, devices[stage])
        copy.start()
        flights.append(copy)

    def step(stage):
        if stage:
            flights[-1].wait_recv()
            totals[stage] = totals[stage - 1] + came[stage - 1]
        if stage < len(devices):
            send(stage)

    def finish():
        for copy in flights:
            copy.wait_send()

    return [lambda stage=stage: step(stage) for stage in range(len(devices) + 1)], finish


def reduce_body(rep_count, shard_count, units, tensors, shorts, *refs):
    planes = len(plane_masks(rep_count, 0))
    order, unpack, vectors, wide_vector, coef_ref, rate_ref, skip_ref, gain_ref, output = refs[:9]
    stored, streams, rest = refs[9:18], refs[18:26], refs[26:]
    sources, rest = list(rest[:3]), rest[3:]
    outs, rest = rest[:tensors], rest[tensors:]
    grads_out, output_out, vectors_out, wide_out = rest[:4]
    rest = rest[4:]
    held, flows, rest = rest[:9], rest[9:17], rest[17:]
    per_kind = planes + 4
    kinds = [rest[:per_kind], (None,) + rest[per_kind : 2 * per_kind - 1]]
    kinds.append((None,) + rest[2 * per_kind - 1 : 3 * per_kind - 2])
    rest = rest[3 * per_kind - 2 :]
    (made, ssm_made, flat, coef_grad, rate_grad, kernel_grad, taps_grad) = rest[:7]
    (grad_q, grad_k, grad_v, grad_b, grads, totals, came_totals, wide, came_wide) = rest[7:16]
    staged, landed, landed_two = rest[16:19]
    send, receive, kept, load_sems, wrote, deal_one, deal_two, sums, flow_sems = rest[19:]
    for i in range(3):
        sources.append(made.at[i])
    sources.append(ssm_made)
    place = Place(rep_count, shard_count)
    place.meet_all()
    count = flights_of(rep_count, shard_count)
    works = []

    def writer(tensor, pick):
        def write(piece, value):
            pltpu.make_async_copy(
                value, pick(outs[tensor].at[piece]), wrote.at[tensor]
            ).start()

        return write

    for index, (tensor, pick, target, kind, slot) in enumerate(units):
        bufs = kinds[kind]
        works.append(
            Reduction(
                place,
                index % 2,
                pick(sources[tensor]),
                None if bufs[0] is None else bufs[0].at[slot],
                [buf.at[slot] for buf in bufs[1 : 1 + planes + 2]],
                bufs[-1].at[slot],
                (send, receive, kept),
                index * count,
                writer(tensor, target),
            )
        )
    todo = [work.steps() for work in works]
    started = [0]

    def start_to(limit):
        while started[0] < min(limit, len(works)):
            works[started[0]].start()
            started[0] += 1

    start_to(REDUCE_AHEAD)
    loads = loads_of(zip(stored, held), load_sems)
    middle, tokens, normed, table, table_t, w_out = held[:6]
    w_qkv = held[6:9]
    tile = flows[0].shape[2]

    def flow(index):
        lanes = pl.ds(index * tile, tile)
        return loads_of(
            [(a.at[:, lanes], b.at[index % 2]) for a, b in zip(streams, flows)],
            flow_sems.at[index],
        )

    flowing = [flow(0), flow(1)]
    deal_start(
        (output,), order, staged, landed, (deal_one.at[0], deal_one.at[1]), place
    )

    rows, channels = middle.shape
    taps = taps_grad.shape[0]
    length = rows - shorts * taps
    totals[0] = vectors[...]
    wide[0] = wide_vector[...]

    def arrive():
        for copy in loads:
            copy.wait()
        grad_b[...] = to_half(middle[...])
        totals[0, 6:7, :] = column_sums(grad_b[...])

    def store_grad(index, left, right):
        parts = shard_count // 2
        wide_rows = channels // 2
        for i in range(2):
            part = dot_tn(left[:, i * wide_rows : (i + 1) * wide_rows], right[...], jnp.bfloat16)
            made[index, i * parts : (i + 1) * parts] = part.reshape(
                (parts,) + made.shape[2:]
            )

    def lags_of(real, imag, out, lags, lanes):
        top_re, top_im = to_half(real[:length] * (1.0 / length)), to_half(imag[:length] * (1.0 / length))
        low_re, low_im = real[length : length + taps], imag[length : length + taps]
        for i in range(1, shorts):
            at = length + i * taps
            low_re, low_im = low_re + real[at : at + taps], low_im + imag[at : at + taps]
        low_re, low_im = to_half(low_re * (1.0 / taps)), to_half(low_im * (1.0 / taps))
        total = dot_nn(table_t[0:lags, 0:length], top_re)
        total = total + dot_nn(table_t[0:lags, rows : rows + length], top_im)
        at = slice(length, length + taps)
        head = dot_nn(table_t[at, at], low_re)
        head = head + dot_nn(table_t[at, rows + length : rows + length + taps], low_im)
        out[0:taps, lanes] = total[:taps] + head
        if lags > taps:
            out[taps:lags, lanes] = total[taps:]

    def mix_job(index):
        lanes = slice(index * tile, (index + 1) * tile)
        for copy in flowing[index]:
            copy.wait()
        queries, values, shifted, mixed, in_wave, key_wave, kernel_wave, taps_wave = [
            ref.at[index % 2] for ref in flows
        ]
        gate = dot_nt(grad_b[...], w_out[lanes, :])
        grad_q[:, lanes] = to_half(gate * to_float(mixed[...]))
        grad = gate * to_float(queries[...])
        wave = dot_nn(table[...], to_half(grad))
        g_re, g_im = wave[:rows], wave[rows:]
        k_re, k_im = to_float(kernel_wave[:rows]), to_float(kernel_wave[rows:])
        back = dot_nn(table_t[:, :rows], to_half(g_re * k_re + g_im * k_im))
        back = back + dot_nn(table_t[:, rows:], to_half(g_im * k_re - g_re * k_im))
        back = back + skip_ref[:, lanes] * grad
        value, moved = to_float(values[...]), to_float(shifted[...])
        totals[0, 5:6, lanes] = jnp.sum(grad * (value * moved), axis=0, keepdims=True)
        u_re, u_im = to_float(in_wave[:rows]), to_float(in_wave[rows:])
        lags_of(g_re * u_re + g_im * u_im, g_im * u_re - g_re * u_im, kernel_grad, length, lanes)
        grad_v[:, lanes] = to_half(back * moved)
        wave = dot_nn(table[...], to_half(back * value))
        s_re, s_im = wave[:rows], wave[rows:]
        t_re, t_im = to_float(taps_wave[:rows]), to_float(taps_wave[rows:])
        back = dot_nn(table_t[:, :rows], to_half(s_re * t_re + s_im * t_im))
        back = back + dot_nn(table_t[:, rows:], to_half(s_im * t_re - s_re * t_im))
        grad_k[:, lanes] = to_half(back)
        x_re, x_im = to_float(key_wave[:rows]), to_float(key_wave[rows:])
        lags_of(s_re * x_re + s_im * x_im, s_im * x_re - s_re * x_im, taps_grad, taps, lanes)
        if (index + 2) * tile < channels:
            flowing.append(flow(index + 2))

    def column_sums(array):
        return jnp.sum(to_float(array), axis=0, keepdims=True)

    def bias_job():
        totals[0, 2:3, :] = column_sums(grad_q[...])
        totals[0, 3:4, :] = column_sums(grad_k[...])
        totals[0, 4:5, :] = column_sums(grad_v[...])

    piece_rows = grads.shape[1]

    def norm_job(tile):
        size = 128
        at = slice(tile * size, tile * size + size)
        error = dot_nt(grad_q[at, :], w_qkv[0][...]) + dot_nt(grad_k[at, :], w_qkv[1][...])
        error = error + dot_nt(grad_v[at, :], w_qkv[2][...])
        hat, scale = row_stats(to_float(tokens[at, :]))
        first = jnp.sum(error * hat, axis=0, keepdims=True)
        second = jnp.sum(error, axis=0, keepdims=True)
        if tile:
            first, second = first + totals[0, 0:1, :], second + totals[0, 1:2, :]
        totals[0, 0:1, :] = first
        totals[0, 1:2, :] = second
        grad = to_half(middle[at, :] + norm_back(error, hat, scale, gain_ref[...]))
        count = size // piece_rows
        grads[tile * count : (tile + 1) * count] = grad.reshape(count, piece_rows, channels)

    def ssm_job(tile):
        lanes = slice(tile * 128, tile * 128 + 128)
        tile_grads(coef_ref, rate_ref, kernel_grad, coef_grad, rate_grad, lanes)
        both = jnp.concatenate([taps_grad[:, lanes], coef_grad[:, lanes]]).T
        last = jnp.concatenate([rate_grad[:, lanes], rate_grad[:, lanes]]).T
        flat[lanes, :] = jnp.concatenate([both, last[:, :taps]], axis=1)

    def fill_job():
        piece = channels // (shard_count * rep_count)
        for i in range(shard_count * rep_count):
            ssm_made[i // rep_count, (i % rep_count) // 2, i % 2] = to_half(
                flat[i * piece : (i + 1) * piece, :]
            )

    def deal_job():
        deal_end(
            (output_out,), unpack, staged, landed, (deal_one.at[0], deal_one.at[1]), place
        )
        deal_start(
            (grads,), order, staged, landed_two, (deal_two.at[0], deal_two.at[1]), place
        )

    vector_steps, vector_end = sum_everywhere(place, totals, came_totals, (sums.at[0], sums.at[1]), 0)
    wide_steps, wide_end = sum_everywhere(
        place, wide, came_wide, (sums.at[0], sums.at[1]), len(vector_steps)
    )
    mixes = [lambda i=i: mix_job(i) for i in range(channels // tile)]
    third = -(-len(mixes) // 3)
    norms = [lambda i=i: norm_job(i) for i in range(rows // 128)]
    ssms = [lambda i=i: ssm_job(i) for i in range(channels // 128)]
    jobs = [
        [arrive] + mixes[:third],
        mixes[third : 2 * third],
        mixes[2 * third :],
        [
            lambda: store_grad(0, normed, grad_q),
            lambda: store_grad(1, normed, grad_v),
            lambda: store_grad(2, normed, grad_k),
            bias_job,
        ],
        norms[:2],
        norms[2:] + [deal_job],
        ssms[:2],
        ssms[2:4],
        ssms[4:] + [fill_job],
    ]
    for i, pair in enumerate(zip(vector_steps, wide_steps)):
        while len(jobs) < 7 + i:
            jobs.append([])
        jobs[6 + i] = list(pair) + jobs[6 + i]
    steps = len(todo[0])
    for step in range(len(works) + (steps - 1) * REDUCE_LAG):
        if step < len(jobs):
            for job in jobs[step]:
                job()
        start_to(step + REDUCE_AHEAD + 1 if step < 8 else len(works))
        for position in range(steps - 1, -1, -1):
            index = step - position * REDUCE_LAG
            if 0 <= index < len(works):
                todo[index][position]()
    deal_end(
        (grads_out,), unpack, staged, landed_two, (deal_two.at[0], deal_two.at[1]), place
    )
    owned = channels // shard_count
    last = len(vector_steps) - 1
    total = totals[last]
    narrow = jnp.zeros((VECTORS, owned), jnp.float32)
    step_wide = wide.shape[2] // shard_count
    total_wide = wide[last]
    chosen = jnp.zeros((1, step_wide), jnp.float32)
    for s in range(shard_count):
        here = place.shard == s
        turned = pltpu.roll(total, (channels - s * owned) % channels, axis=1) if s else total
        narrow = narrow + jnp.where(here, turned[:, :owned], 0.0)
        chosen = chosen + jnp.where(here, total_wide[:, s * step_wide : (s + 1) * step_wide], 0.0)
    vectors_out[...] = narrow
    wide_out[...] = chosen
    vector_end()
    wide_end()
    for work in works:
        work.finish()
    for tensor in range(tensors):
        pltpu.make_async_copy(outs[tensor], outs[tensor], wrote.at[tensor]).wait()


def reduce_all(
    order, unpack, vectors, wide, rows_in, output, stored, streams, down, up, square, counts, shorts
):
    rep_count, shard_count = counts
    slots = rep_count * shard_count
    rows, width = output.shape
    piece = width // slots
    parts = up.shape[1] // width
    lead = (shard_count, rep_count // 2, 2)
    tensors = [down.reshape(lead + (parts, piece, width)), up.reshape(lead + (piece, up.shape[1]))]
    tensors.append(square.reshape(lead + (piece, width)))
    states, channels = rows_in[0].shape
    length = rows - shorts * states
    outs = [jax.ShapeDtypeStruct((rep_count, parts, piece, width), jnp.bfloat16)]
    outs.append(jax.ShapeDtypeStruct((rep_count, piece, up.shape[1]), jnp.bfloat16))
    outs += [jax.ShapeDtypeStruct((rep_count, piece, width), jnp.bfloat16)] * 4
    outs.append(jax.ShapeDtypeStruct((rep_count, piece, 3 * states), jnp.bfloat16))
    plain_outs = len(outs)
    piece_shape = (slots, rows // slots, width)
    outs += [jax.ShapeDtypeStruct(piece_shape, output.dtype)] * 2
    outs.append(jax.ShapeDtypeStruct((VECTORS, width // shard_count), jnp.float32))
    outs.append(jax.ShapeDtypeStruct((1, wide.shape[1] // shard_count), jnp.float32))

    def whole(ref):
        return ref

    units = []
    for q in range(parts):
        units.append(
            (0, lambda ref, q=q: ref.at[:, :, :, q], lambda ref, q=q: ref.at[q], 0, len(units))
        )
    for q in range(parts):
        units.append(
            (
                1,
                lambda ref, q=q: ref.at[:, :, :, :, pl.ds(q * width, width)],
                lambda ref, q=q: ref.at[:, pl.ds(q * width, width)],
                0,
                len(units),
            )
        )
    units.append((2, whole, whole, 0, len(units)))
    plain = len(units)
    for i in range(3):
        units.append((3 + i, whole, whole, 1, i))
    units.append((6, whole, whole, 2, 0))
    half = rep_count // 2
    planes = len(plane_masks(rep_count, 0))

    def buffers(count, rows, columns, kept):
        shapes = [(shard_count, half)] * (2 if kept else 1)
        size = half
        for _ in range(planes):
            size //= 2
            shapes.append((size, shard_count))
        shapes += [(shard_count - 1,), (rep_count,)]
        return [pltpu.VMEM((count,) + shape + (rows, columns), jnp.bfloat16) for shape in shapes]

    tile = 128 if piece % 8 else 256
    flights = len(units) * flights_of(rep_count, shard_count)
    stages = slots.bit_length()
    anywhere = pl.BlockSpec(memory_space=pl.ANY)
    here = pl.BlockSpec(memory_space=pltpu.VMEM)
    scalars = pl.BlockSpec(memory_space=pltpu.SMEM)
    found = pl.pallas_call(
        lambda *refs: reduce_body(rep_count, shard_count, units, plain_outs, shorts, *refs),
        in_specs=[scalars] * 2 + [here] * 7 + [anywhere] * (len(stored) + len(streams) + 3),
        out_specs=[anywhere] * plain_outs + [here] * 4,
        out_shape=outs,
        scratch_shapes=[pltpu.VMEM(array.shape, array.dtype) for array in stored]
        + [pltpu.VMEM((2, array.shape[0], tile), array.dtype) for array in streams]
        + buffers(plain, piece, width, True)
        + buffers(3, piece, width, False)
        + buffers(1, piece, 3 * states, False)
        + [
            pltpu.VMEM((3,) + lead + (piece, width), jnp.bfloat16),
            pltpu.VMEM(lead + (piece, 3 * states), jnp.bfloat16),
            pltpu.VMEM((channels, 3 * states), jnp.float32),
            pltpu.VMEM((states, channels), jnp.float32),
            pltpu.VMEM((states, channels), jnp.float32),
            pltpu.VMEM((length, channels), jnp.float32),
            pltpu.VMEM((states, channels), jnp.float32),
        ]
        + [pltpu.VMEM((rows, width), jnp.bfloat16)] * 4
        + [
            pltpu.VMEM(piece_shape, jnp.bfloat16),
            pltpu.VMEM((stages, VECTORS, width), jnp.float32),
            pltpu.VMEM((stages - 1, VECTORS, width), jnp.float32),
            pltpu.VMEM((stages, 1, wide.shape[1]), jnp.float32),
            pltpu.VMEM((stages - 1, 1, wide.shape[1]), jnp.float32),
        ]
        + [pltpu.VMEM((slots, 1) + piece_shape[1:], jnp.bfloat16)] * 3
        + [pltpu.SemaphoreType.DMA((flights,))] * 3
        + [
            pltpu.SemaphoreType.DMA((len(stored),)),
            pltpu.SemaphoreType.DMA((plain_outs,)),
            pltpu.SemaphoreType.DMA((2, slots)),
            pltpu.SemaphoreType.DMA((2, slots)),
            pltpu.SemaphoreType.DMA((2, 2 * stages)),
            pltpu.SemaphoreType.DMA((width // tile, len(streams))),
        ],
        compiler_params=pltpu.CompilerParams(
            collective_id=1, has_side_effects=True, vmem_limit_bytes=63 * 1024 * 1024
        ),
        cost_estimate=pl.CostEstimate(flops=0, bytes_accessed=200_000_000, transcendentals=0),
        name="reduce_all",
    )(order, unpack, vectors, wide, *rows_in, output.reshape(piece_shape), *stored, *streams, *tensors)
    own = rep_count * piece
    return (
        found[plain_outs].reshape(output.shape),
        found[plain_outs + 1].reshape(output.shape),
        to_float(found[0].reshape(own * parts, width)),
        to_float(found[1].reshape(own, up.shape[1])),
        [to_float(g.reshape(own, width)) for g in found[2:6]],
        to_float(found[6].reshape(own, 3 * states)),
        found[plain_outs + 2],
        found[plain_outs + 3],
    )


def row_stats(values):
    average = jnp.mean(values, axis=-1, keepdims=True)
    centred = values - average
    spread = jnp.mean(centred * centred, axis=-1, keepdims=True)
    scale = lax.rsqrt(spread + EPSILON)
    return centred * scale, scale


def norm_back(error, hat, scale, gain):
    pulled = error * gain
    return scale * (
        pulled
        - jnp.mean(pulled, axis=-1, keepdims=True)
        - hat * jnp.mean(pulled * hat, axis=-1, keepdims=True)
    )


def column_sum(array):
    return jnp.sum(to_float(array), axis=0)


def local(
    tokens,
    ln1_scale,
    ln1_shift,
    w_query,
    b_query,
    w_key,
    b_key,
    w_value,
    b_value,
    shift_taps,
    ssm_coef,
    ssm_rate,
    ssm_skip,
    w_out,
    b_out,
    ln2_scale,
    ln2_shift,
    w_up,
    b_up,
    w_down,
    b_down,
    cotangent,
    piece_slot,
    lengths,
):
    rep_count, shard_count = lax.axis_size("rep"), lax.axis_size("shard")
    slots = rep_count * shard_count
    me = lax.axis_index("rep") * shard_count + lax.axis_index("shard")
    rows, width = tokens.shape
    piece_rows = rows // slots
    taps = shift_taps.shape[1]
    blocks = rows // taps
    owned = ssm_skip.shape[0]
    shorts = lengths.shape[1] - 1
    long_blocks = blocks - shorts
    per_block = slots // blocks

    ids = jnp.arange(slots, dtype=jnp.int32)
    table = piece_slot.reshape(slots, slots)
    target = table // slots
    arrival = jnp.sum(jnp.where(target == me, table % slots, 0), axis=1)
    own_target = jnp.sum(jnp.where(ids[:, None] == me, target, 0), axis=0)
    sizes = lengths[0] // taps
    starts = jnp.cumsum(sizes) - sizes
    first = jnp.sum(jnp.where(sizes == long_blocks, starts, 0))
    block = arrival // per_block
    moved = jnp.where(
        block < first,
        block + long_blocks,
        jnp.where(block < first + long_blocks, block - first, block),
    )
    arrival = moved * per_block + arrival % per_block
    sending = jnp.sum(jnp.where(own_target[None, :] == ids[:, None], ids[None, :], 0), axis=1)
    unpacking = jnp.sum(jnp.where(arrival[None, :] == ids[:, None], ids[None, :], 0), axis=1)

    pack = jnp.concatenate(
        [
            vector.reshape(1, owned)
            for vector in (
                ln1_scale,
                ln1_shift,
                b_query,
                b_key,
                b_value,
                ssm_skip,
                b_out,
                ln2_scale,
                ln2_shift,
                b_down,
            )
        ]
        + [b_up.reshape(-1, owned)]
    )
    counts = (rep_count, shard_count)
    weights, packs, balanced_low, grad_low, spectra = gather_all(
        sending,
        unpacking,
        tokens,
        cotangent,
        [w_query, w_key, w_value, w_out],
        w_up,
        w_down,
        pack,
        [shift_taps, ssm_coef, ssm_rate],
        counts,
        shorts,
    )
    weight_q, weight_k, weight_v, weight_o, weight_up, weight_down = weights
    kernel_wave, taps_wave, table, table_t, coef_rows, rate_rows = spectra
    balanced = to_float(balanced_low)
    up_bias = to_float(packs[:, 10:].reshape(1, -1))
    small = to_float(jnp.swapaxes(packs[:, :10], 0, 1).reshape(10, width))
    (
        gain_one,
        bias_one,
        query_bias,
        key_bias,
        value_bias,
        skip,
        out_bias,
        gain_two,
        bias_two,
        down_bias,
    ) = [small[i : i + 1] for i in range(10)]

    half = rows

    def times(wave, filter_wave):
        real, imag = wave[:half], wave[half:]
        f_re, f_im = to_float(filter_wave[:half]), to_float(filter_wave[half:])
        return jnp.concatenate(
            [to_half(real * f_re - imag * f_im), to_half(real * f_im + imag * f_re)]
        )

    hat_one, scale_one = row_stats(balanced)
    normed = to_half(hat_one * gain_one + bias_one)
    queries = dot_nn(normed, weight_q) + query_bias
    keys = to_half(dot_nn(normed, weight_k) + key_bias)
    values = dot_nn(normed, weight_v) + value_bias
    key_wave = dot_nn(table, keys)
    shifted = dot_nn(table_t, times(key_wave, taps_wave))
    inputs = shifted * values
    in_wave = dot_nn(table, to_half(inputs))
    mixed = dot_nn(table_t, times(in_wave, kernel_wave)) + skip * inputs
    gated = to_half(queries * mixed)
    middle = balanced + (dot_nn(gated, weight_o) + out_bias)
    hat_two, scale_two = row_stats(middle)
    normed_two = to_half(hat_two * gain_two + bias_two)

    hidden = dot_nn(normed_two, weight_up) + up_bias
    bent = jnp.tanh(GELU_A * (hidden + GELU_B * hidden * hidden * hidden))
    active = to_half(0.5 * hidden * (1.0 + bent))
    slope = 0.5 * (1.0 + bent) + 0.5 * hidden * (1.0 - bent * bent) * GELU_A * (
        1.0 + 3.0 * GELU_B * hidden * hidden
    )
    branch = dot_nn(active, weight_down)
    result = middle + (branch + down_bias)
    output = to_half(result)

    grad_out = to_float(grad_low)
    part_down = dot_tn(active, grad_low, jnp.bfloat16)
    g_b_down = column_sum(grad_low)
    grad_hidden = to_half(dot_nt(grad_low, weight_down) * slope)
    part_up = dot_tn(normed_two, grad_hidden, jnp.bfloat16)
    g_b_up = column_sum(grad_hidden)
    error = dot_nt(grad_hidden, weight_up)
    g_ln2_scale = jnp.sum(error * hat_two, axis=0)
    g_ln2_shift = jnp.sum(error, axis=0)
    grad_middle = grad_out + norm_back(error, hat_two, scale_two, gain_two)
    vectors = jnp.concatenate(
        [
            jnp.zeros((7, width), jnp.float32),
            g_ln2_scale[None],
            g_ln2_shift[None],
            g_b_down[None],
            jnp.zeros((VECTORS - 10, width), jnp.float32),
        ]
    )
    grad_tokens, block_output, grad_w_down, grad_w_up, squares, ssm, vec, wide = reduce_all(
        arrival,
        own_target,
        vectors,
        g_b_up[None],
        [coef_rows, rate_rows, skip, gain_one],
        output,
        [
            grad_middle,
            balanced_low,
            normed,
            table,
            table_t,
            weight_o,
            weight_q,
            weight_k,
            weight_v,
        ],
        [
            to_half(queries),
            to_half(values),
            to_half(shifted),
            to_half(mixed),
            to_half(in_wave),
            to_half(key_wave),
            kernel_wave,
            taps_wave,
        ],
        part_down,
        part_up,
        dot_tn(gated, to_half(grad_middle), jnp.bfloat16),
        counts,
        shorts,
    )
    grad_w_out, grad_w_query, grad_w_value, grad_w_key = squares
    return (
        block_output,
        grad_tokens,
        vec[0],
        vec[1],
        grad_w_query,
        vec[2],
        grad_w_key,
        vec[3],
        grad_w_value,
        vec[4],
        ssm[:, :taps],
        ssm[:, taps : 2 * taps],
        ssm[:, 2 * taps :],
        vec[5],
        grad_w_out,
        vec[6],
        vec[7],
        vec[8],
        grad_w_up,
        wide[0],
        grad_w_down,
        vec[9],
    )


def solution(mesh):
    both = P(("rep", "shard"), None)
    row, mat = P("shard"), P("shard", None)
    in_specs = (
        (both, row, row, mat, row, mat, row, mat, row, mat, mat, mat, row)
        + (mat, row, row, row, mat, row, mat, row, both, P(), both)
    )
    out_specs = (
        (both, both, row, row, mat, row, mat, row, mat, row, mat, mat, mat, row)
        + (mat, row, row, row, mat, row, mat, row)
    )
    return jax.shard_map(local, mesh=mesh, in_specs=in_specs, out_specs=out_specs, check_vma=False)
```
